32 devices in a mesh: group: 2 (over y), ctx: 4 (over z), smp: 2 (over x), head: 2 (over core).
Axes of the slice: x: 2, y: 2, z: 4, core: 2. Of those that a mesh axis runs over, the one named last changes fastest.
Arguments:
- queries: bfloat16 [512, 2, 4096], P(('group', 'smp'), 'head'), parts along dimension 0, may hold values from -8 to 8
- prefix_cache: bfloat16 [2, 8192, 2, 512], P(None, ('group', 'ctx'), 'head'), parts along dimension 1, may hold values from -8 to 8
- suffix_cache: bfloat16 [2, 512, 128, 2, 512], P(None, ('group', 'ctx', 'smp'), None, 'head'), parts along dimension 1, may hold values from -8 to 8
- suffix_length: int32 [512], P(('group', 'smp')), parts along dimension 0, may hold values from 1 to 128, as said below
- cache_sample: int32 [512], P('group'), parts along dimension 0, may hold values from 0 to 255, as said below
- residual: bfloat16 [512, 8192], P(('group', 'ctx', 'head'), 'smp'), parts along dimension 0, may hold values from -6 to 6
- w_out: bfloat16 [2, 4096, 8192], P('head', 'ctx', 'smp'), may hold values from -0.75 to 0.75
- norm_gain: float32 [8192], P('smp'), may hold values from 0.1 to 1.9
- gate_matrix: bfloat16 [8192, 16384], P('smp', ('ctx', 'head')), may hold values from -0.0625 to 0.0625
- w_up: bfloat16 [8192, 16384], P('smp', ('ctx', 'head')), may hold values from -0.0625 to 0.0625
- w_down: bfloat16 [16384, 8192], P(('ctx', 'head'), 'smp'), may hold values from -0.046875 to 0.046875
Outputs:
- mixed: bfloat16 [512, 8192], P(('group', 'ctx', 'head'), 'smp'), parts along dimension 0
The draws below stay inside these ranges and needn't reach their ends.
There are 2 independent parts, one for each index of `group`. The reference program is written for one: setup_inputs(seed, part) draws one part's arguments, and reference() takes and returns one part's arrays. A program takes and returns all parts, laid end to end along the dimension named above; an argument that names none is the same for every part. Nothing has to cross between parts.
Inputs may be any that keep to these rules, and one draw needn't show every extreme that they name: `suffix_length`: the longest is exactly 128 in every draw. A permutation; cache row r and sample cache_sample[r] lie in the same group, the group of row r being (r // 32) % (2) and that of sample i being i // 128.
All inputs are finite; a program needn't handle non-finite values.
Results may differ from the reference program's by a relative error of at most 0.012.
Values may be sent and summed in bfloat16 or wider, within the bound.
A program may use at most 192 MiB of HBM per device.

```python
import jax
import jax.numpy as jnp
from jax import lax

D = 8192
QUERY_HEADS = 64
KEY_VALUE_HEADS = 8
HD = 128
FF = 16384
SAMP_GRP = 128
PRE_DEV = 1024
SUFFIX = 128
HEAD_GROUP_COUNT = 2
QW = 4096
KVW = 512
PREFIX = 4096
SAMPLES = 256
ROWS_DEV = 32
N_CTX = 4


def drawn_draw(key):
    query_key = jax.random.fold_in(key, 11)
    cache_key = jax.random.fold_in(key, 12)
    value_key = jax.random.fold_in(key, 13)
    query_shape = (SAMPLES, HEAD_GROUP_COUNT, QW)
    cache_shape = (PREFIX, HEAD_GROUP_COUNT, KVW)
    queries = jnp.clip(jax.random.normal(query_key, query_shape, jnp.float32), -6.0, 6.0)
    prefix_keys = jnp.clip(1.5 * jax.random.normal(cache_key, cache_shape, jnp.float32), -8.0, 8.0)
    prefix_values = jnp.clip(jax.random.normal(value_key, cache_shape, jnp.float32), -6.0, 6.0)
    return (queries, jnp.stack([prefix_keys, prefix_values]))


def draw_queries(key, part):
    return drawn_draw(key)[0].astype(jnp.bfloat16)


def draw_prefix_cache(key, part):
    return drawn_draw(key)[1].astype(jnp.bfloat16)


def draw_suffix_length(key, part):
    lengths = jax.random.randint(jax.random.fold_in(key, 21), (SAMPLES,), 1, SUFFIX + 1)
    longest = jax.random.randint(jax.random.fold_in(key, 22), (), 0, SAMPLES)
    return lengths.at[longest].set(SUFFIX).astype(jnp.int32)


def draw_cache_sample(key, part):
    groups = SAMPLES // SAMP_GRP
    row_ids = jnp.arange(SAMPLES, dtype=jnp.int32)
    group_of_row = row_ids // ROWS_DEV % groups
    rank = row_ids // (ROWS_DEV * groups) * ROWS_DEV + row_ids % ROWS_DEV
    orders = jnp.stack([jax.random.permutation(jax.random.fold_in(key, 31 + number), SAMP_GRP) for number in range(groups)])
    return (group_of_row * SAMP_GRP + orders[group_of_row, rank]).astype(jnp.int32)


def draw_suffix_cache(key, part):
    cache_shape = (2, SAMPLES, SUFFIX, HEAD_GROUP_COUNT, KVW)
    cache_key = jax.random.fold_in(key, 41)
    cache = jnp.clip(3.0 * jax.random.normal(cache_key, cache_shape, jnp.float32), -5.0, 5.0)
    return cache.astype(jnp.bfloat16)


def levels(stream_key, dims, cuts, smallest, top_value):
    factor_of = 1.0
    for axis_at, blocks in cuts:
        draws = jax.random.uniform(jax.random.fold_in(jax.random.fold_in(stream_key, 6), axis_at), (blocks,), jnp.float32, smallest / len(cuts), top_value / len(cuts))
        factor_of = factor_of * jnp.repeat(jnp.exp(draws), dims[axis_at] // blocks).reshape((-1,) + (1,) * (len(dims) - 1 - axis_at))
    return factor_of


def normal_values(own_key, extent, spread, limit, pieces=(), kind=jnp.bfloat16):
    entries = spread * jax.random.normal(own_key, extent, jnp.float32)
    if pieces:
        entries = entries * levels(own_key, extent, pieces, -0.22, 0.18)
    return jnp.clip(entries, -limit, limit).astype(kind)


def setup_inputs(seed: int = 0, part: int = 0) -> dict:
    arg_keys = jax.random.split(jax.random.key(seed), 12)
    part_splits = jax.random.split(jax.random.fold_in(arg_keys[11], part), 12)
    return {
        "queries": draw_queries(jax.random.fold_in(jax.random.fold_in(arg_keys[11], part), 71), part),
        "prefix_cache": draw_prefix_cache(jax.random.fold_in(jax.random.fold_in(arg_keys[11], part), 71), part),
        "suffix_cache": draw_suffix_cache(jax.random.fold_in(jax.random.fold_in(arg_keys[11], part), 71), part),
        "suffix_length": draw_suffix_length(jax.random.fold_in(jax.random.fold_in(arg_keys[11], part), 71), part),
        "cache_sample": draw_cache_sample(jax.random.fold_in(jax.random.fold_in(arg_keys[11], part), 71), part),
        "residual": normal_values(part_splits[5], (SAMPLES, D), 1.0, 6.0, ((0, 8), (1, 2))),
        "w_out": normal_values(arg_keys[6], (HEAD_GROUP_COUNT, QW, D), (QUERY_HEADS * HD // 128) ** -0.5, 0.75, ((0, 2), (1, 4), (2, 2))),
        "norm_gain": jnp.clip(1.0 + 0.18 * jax.random.normal(arg_keys[7], (D,), jnp.float32), 0.1, 1.9),
        "gate_matrix": normal_values(arg_keys[8], (D, FF), D ** -0.5, 0.0625, ((0, 2), (1, 8))),
        "w_up": normal_values(arg_keys[9], (D, FF), D ** -0.5, 0.0625, ((0, 2), (1, 8))),
        "w_down": normal_values(arg_keys[10], (FF, D), FF ** -0.5, 0.046875, ((0, 8), (1, 2))),
    }


EPSILON = 1e-05

def finish_piece(scores, values, form):
    highest = lax.optimization_barrier(jnp.max(scores, axis=-1))
    weights = jnp.exp(scores - highest[..., None])
    totals = lax.optimization_barrier(jnp.sum(weights, axis=-1))
    rounded = lax.optimization_barrier(weights.astype(jnp.bfloat16)).astype(jnp.float32)
    summed = jnp.einsum(form, rounded, values)
    piece_out = (summed / totals[..., None]).astype(jnp.bfloat16)
    return (piece_out, highest + jnp.log(totals))

def reference(queries, prefix_cache, suffix_cache, suffix_length, cache_sample, residual, w_out, norm_gain, gate_matrix, w_up, w_down):
    key_value_heads_here = KEY_VALUE_HEADS // HEAD_GROUP_COUNT
    queries_per_key_value = QUERY_HEADS // KEY_VALUE_HEADS
    score_scale = HD ** (-0.5)
    query_rows = queries.astype(jnp.float32).reshape(SAMPLES, HEAD_GROUP_COUNT, key_value_heads_here, queries_per_key_value, HD)
    prefix_keys = prefix_cache[0].astype(jnp.float32).reshape(PREFIX, HEAD_GROUP_COUNT, key_value_heads_here, HD)
    prefix_values = prefix_cache[1].astype(jnp.float32).reshape(PREFIX, HEAD_GROUP_COUNT, key_value_heads_here, HD)

    def block_piece(block):
        start_pos = (block * PRE_DEV).astype(jnp.int32)
        block_keys = lax.dynamic_slice_in_dim(prefix_keys, start_pos, PRE_DEV, 0)
        block_values = lax.dynamic_slice_in_dim(prefix_values, start_pos, PRE_DEV, 0)
        scores = jnp.einsum('shjgd,phjd->shjgp', query_rows, block_keys) * score_scale
        return finish_piece(scores, block_values, 'shjgp,phjd->shjgd')
    block_out, block_lse = lax.map(block_piece, jnp.arange(N_CTX, dtype=jnp.int32))
    row_of = jnp.zeros((SAMPLES,), jnp.int32).at[cache_sample].set(jnp.arange(SAMPLES, dtype=jnp.int32))
    own_cache = jnp.take(suffix_cache, row_of, axis=1)
    suffix_keys = own_cache[0].astype(jnp.float32).reshape(SAMPLES, SUFFIX, HEAD_GROUP_COUNT, key_value_heads_here, HD)
    suffix_values = own_cache[1].astype(jnp.float32).reshape(SAMPLES, SUFFIX, HEAD_GROUP_COUNT, key_value_heads_here, HD)
    suffix_scores = jnp.einsum('shjgd,sthjd->shjgt', query_rows, suffix_keys) * score_scale
    positions = lax.broadcasted_iota(jnp.int32, suffix_scores.shape, 4)
    live = positions < suffix_length.astype(jnp.int32)[:, None, None, None, None]
    suffix_scores = jnp.where(live, suffix_scores, -jnp.inf)
    suffix_out, suffix_lse = finish_piece(suffix_scores, suffix_values, 'shjgt,sthjd->shjgd')
    all_out = jnp.concatenate([block_out, suffix_out[None]], axis=0)
    all_out = lax.optimization_barrier(all_out).astype(jnp.float32)
    all_lse = jnp.concatenate([block_lse, suffix_lse[None]], axis=0)
    top = lax.optimization_barrier(jnp.max(all_lse, axis=0))
    piece_weights = jnp.exp(all_lse - top[None])
    numer = lax.optimization_barrier(jnp.sum(piece_weights[..., None] * all_out, axis=0))
    denom = lax.optimization_barrier(jnp.sum(piece_weights, axis=0))
    attention = (numer / denom[..., None]).astype(jnp.bfloat16).reshape(SAMPLES, HEAD_GROUP_COUNT * QW)
    projected = jnp.dot(attention, w_out.reshape(HEAD_GROUP_COUNT * QW, D), preferred_element_type=jnp.float32)
    state = (residual.astype(jnp.float32) + projected).astype(jnp.bfloat16)
    state_wide = lax.optimization_barrier(state).astype(jnp.float32)
    inverse_rms = lax.rsqrt(lax.optimization_barrier(jnp.mean(state_wide * state_wide, axis=1)) + EPSILON)
    scaled = (state_wide * norm_gain).astype(jnp.bfloat16)
    gate = inverse_rms[:, None] * jnp.dot(scaled, gate_matrix, preferred_element_type=jnp.float32)
    up_part = inverse_rms[:, None] * jnp.dot(scaled, w_up, preferred_element_type=jnp.float32)
    hidden = (jax.nn.silu(gate) * up_part).astype(jnp.bfloat16)
    return (state_wide + jnp.dot(hidden, w_down, preferred_element_type=jnp.float32)).astype(jnp.bfloat16)
```

```python
import functools

import jax
import jax.numpy as jnp
from jax import lax
from jax.experimental import pallas as pl
from jax.experimental.pallas import tpu as pltpu
from jax.sharding import PartitionSpec as P

D = 8192
QUERY_HEADS = 64
KEY_VALUE_HEADS = 8
HD = 128


EPSILON = 1e-05


def suffix_piece(row_queries, suffix_cache, row_lengths, key_value_heads_here, score_scale):
    rows_here = suffix_cache.shape[1]
    suffix_keys = suffix_cache[0].reshape(rows_here, -1, key_value_heads_here, HD)
    suffix_values = suffix_cache[1].reshape(rows_here, -1, key_value_heads_here, HD)
    row_scores = (
        jnp.einsum("rjgd,rtjd->rjgt", row_queries, suffix_keys, preferred_element_type=jnp.float32)
        * score_scale
    )
    positions = lax.broadcasted_iota(jnp.int32, row_scores.shape, 3)
    row_scores = jnp.where(positions < row_lengths[:, None, None, None], row_scores, -jnp.inf)
    row_high = jnp.max(row_scores, axis=3)
    row_weights = jnp.exp(row_scores - row_high[..., None])
    row_totals = jnp.sum(row_weights, axis=3)
    row_summed = jnp.einsum(
        "rjgt,rtjd->rjgd",
        row_weights.astype(jnp.bfloat16),
        suffix_values,
        preferred_element_type=jnp.float32,
    )
    row_output = (row_summed / row_totals[..., None]).astype(jnp.bfloat16)
    return (row_output, row_high + jnp.log(row_totals))


MESH = pl.DeviceIdType.MESH
TILE = 512
VMEM_BYTES = 62 * 1024 * 1024


def remote(src, dst, send_sem, recv_sem, where):
    return pltpu.make_async_remote_copy(
        src_ref=src,
        dst_ref=dst,
        send_sem=send_sem,
        recv_sem=recv_sem,
        device_id=where,
        device_id_type=MESH,
    )


def greet(n, n_smp, c, s, h):
    barrier = pltpu.get_barrier_semaphore()
    for k in range(1, n):
        pl.semaphore_signal(barrier, inc=1, device_id={"ctx": lax.rem(c + k, n)}, device_id_type=MESH)
    for k in range(1, n_smp):
        pl.semaphore_signal(
            barrier, inc=1, device_id={"smp": lax.rem(s + k, n_smp)}, device_id_type=MESH
        )
    pl.semaphore_signal(barrier, inc=1, device_id={"head": 1 - h}, device_id_type=MESH)
    pl.semaphore_wait(barrier, (n - 1) + (n_smp - 1) + 1)


class Scatter:
    def __init__(self, n, c, h, buf_a, recv_a, buf_b, recv_b, sa, ra, sb, rb):
        self.n, self.c, self.h = n, c, h
        self.buf_a, self.recv_a, self.buf_b, self.recv_b = buf_a, recv_a, buf_b, recv_b
        self.sa, self.ra, self.sb, self.rb = sa, ra, sb, rb

    def pair_copy(self, t):
        return remote(
            self.buf_a.at[t, 1 - self.h],
            self.recv_a.at[t],
            self.sa.at[t],
            self.ra.at[t],
            {"head": 1 - self.h},
        )

    def row_copy(self, t, k):
        d = lax.rem(self.c + k, self.n)
        return remote(
            self.buf_b.at[t, d],
            self.recv_b.at[t, k - 1],
            self.sb.at[t, k - 1],
            self.rb.at[t, k - 1],
            {"ctx": d},
        )

    def give(self, t, value):
        _, _, n, rows, width = self.buf_a.shape
        parts = value.reshape(n, 2, rows, width).astype(jnp.bfloat16)
        self.buf_a[t, 0] = parts[:, 0]
        self.buf_a[t, 1] = parts[:, 1]
        self.pair_copy(t).start()

    def middle(self, t):
        self.pair_copy(t).wait()
        both = self.buf_a[t, self.h].astype(jnp.float32) + self.recv_a[t].astype(jnp.float32)
        self.buf_b[t] = both.astype(jnp.bfloat16)
        for k in range(1, self.n):
            self.row_copy(t, k).start()

    def finish(self, t):
        total = self.buf_b[t, self.c].astype(jnp.float32)
        for k in range(1, self.n):
            self.row_copy(t, k).wait()
            total = total + self.recv_b[t, k - 1].astype(jnp.float32)
        return total


def columns(t, width):
    return pl.ds(pl.multiple_of(t * width, width), width)


def proj_kernel(
    n,
    n_smp,
    out_ref,
    lse_ref,
    w_ref,
    res_ref,
    state_ref,
    out_in,
    lse_in,
    attn,
    w_buf,
    buf_a,
    recv_a,
    buf_b,
    recv_b,
    w_sem,
    os,
    orr,
    ls,
    lr,
    xs,
    xr,
    sa,
    ra,
    sb,
    rb,
    gs,
    gr,
    fs,
    fr,
):
    c, s, h = lax.axis_index("ctx"), lax.axis_index("smp"), lax.axis_index("head")
    tiles = w_buf.shape[0]

    def w_copy(t):
        return pltpu.make_async_copy(w_ref.at[:, columns(t, TILE)], w_buf.at[t], w_sem.at[t])

    @pl.loop(0, tiles)
    def _(t):
        w_copy(t).start()

    greet(n, n_smp, c, s, h)

    def piece_copies(k):
        d = lax.rem(c + k, n)
        return (
            remote(out_ref.at[d], out_in.at[k - 1], os.at[k - 1], orr.at[k - 1], {"ctx": d}),
            remote(lse_ref.at[d], lse_in.at[k - 1], ls.at[k - 1], lr.at[k - 1], {"ctx": d}),
        )

    for k in range(1, n):
        for copy in piece_copies(k):
            copy.start()
    for k in range(1, n):
        for copy in piece_copies(k):
            copy.wait()

    lses = [lse_ref[c]] + [lse_in[k] for k in range(n - 1)]
    peak = functools.reduce(jnp.maximum, lses)
    scales = [jnp.exp(value - peak) for value in lses]
    denom = functools.reduce(jnp.add, scales)
    scales = [value / denom for value in scales]
    for j in range(lse_ref.shape[2]):
        lanes = slice(j * HD, (j + 1) * HD)
        total = scales[0][:, j : j + 1] * out_ref[c, :, lanes].astype(jnp.float32)
        for k in range(n - 1):
            total = total + scales[k + 1][:, j : j + 1] * out_in[k, :, lanes].astype(jnp.float32)
        attn[s, :, lanes] = total.astype(jnp.bfloat16)

    def attn_copy(k):
        return remote(
            attn.at[s], attn.at[s], xs.at[k - 1], xr.at[k - 1], {"smp": lax.rem(s + k, n_smp)}
        )

    for k in range(1, n_smp):
        attn_copy(k).start()
    for k in range(1, n_smp):
        attn_copy(k).wait()

    scatter = Scatter(n, c, h, buf_a, recv_a, buf_b, recv_b, sa, ra, sb, rb)

    @pl.loop(0, tiles)
    def _(t):
        w_copy(t).wait()
        rows = attn[...].reshape(-1, attn.shape[2])
        scatter.give(t, jnp.dot(rows, w_buf[t], preferred_element_type=jnp.float32))

        @pl.when(t >= 1)
        def _():
            scatter.middle(t - 1)

    scatter.middle(tiles - 1)

    def gather_copy(t, k):
        block = state_ref.at[c, h, :, columns(t, TILE)]
        return remote(
            block, block, gs.at[t, k - 1], gr.at[t, k - 1], {"ctx": lax.rem(c + k, n)}
        )

    def pass_copy(t, k):
        block = state_ref.at[lax.rem(c + n - k, n), h, :, columns(t, TILE)]
        return remote(block, block, fs.at[t, k], fr.at[t, k], {"head": 1 - h})

    @pl.loop(0, tiles)
    def _(t):
        own = scatter.finish(t) + res_ref[:, columns(t, TILE)].astype(jnp.float32)
        state_ref[c, h, :, columns(t, TILE)] = own.astype(jnp.bfloat16)
        for k in range(1, n):
            gather_copy(t, k).start()
        pass_copy(t, 0).start()

    @pl.loop(0, tiles)
    def _(t):
        for k in range(1, n):
            gather_copy(t, k).wait()
            pass_copy(t, k).start()

    @pl.loop(0, tiles)
    def _(t):
        for k in range(n):
            pass_copy(t, k).wait()


def project(n, n_smp, out, lse, w, residual):
    count, group_rows, features = out.shape
    rows, width = residual.shape
    tiles = width // TILE
    vmem = pl.BlockSpec(memory_space=pltpu.VMEM)
    dma = pltpu.SemaphoreType.DMA
    bf16 = jnp.bfloat16
    return pl.pallas_call(
        functools.partial(proj_kernel, n, n_smp),
        out_shape=jax.ShapeDtypeStruct((n, 2, rows, width), bf16),
        in_specs=[vmem, vmem, pl.BlockSpec(memory_space=pl.ANY), vmem],
        out_specs=vmem,
        scratch_shapes=[
            pltpu.VMEM((n - 1, group_rows, features), bf16),
            pltpu.VMEM((n - 1,) + lse.shape[1:], jnp.float32),
            pltpu.VMEM((n_smp, group_rows, features), bf16),
            pltpu.VMEM((tiles, w.shape[0], TILE), bf16),
            pltpu.VMEM((tiles, 2, n, rows, TILE), bf16),
            pltpu.VMEM((tiles, n, rows, TILE), bf16),
            pltpu.VMEM((tiles, n, rows, TILE), bf16),
            pltpu.VMEM((tiles, n - 1, rows, TILE), bf16),
            dma((tiles,)),
            dma((n - 1,)),
            dma((n - 1,)),
            dma((n - 1,)),
            dma((n - 1,)),
            dma((n_smp - 1,)),
            dma((n_smp - 1,)),
            dma((tiles,)),
            dma((tiles,)),
            dma((tiles, n - 1)),
            dma((tiles, n - 1)),
            dma((tiles, n - 1)),
            dma((tiles, n - 1)),
            dma((tiles, n)),
            dma((tiles, n)),
        ],
        compiler_params=pltpu.CompilerParams(
            collective_id=0, has_side_effects=True, vmem_limit_bytes=VMEM_BYTES
        ),
    )(out, lse, w, residual)


UNITS = 256
SLOTS = 4


def ffn_kernel(
    n,
    n_smp,
    state_ref,
    gain_ref,
    gate_ref,
    up_ref,
    down_ref,
    mixed_ref,
    scaled,
    squares,
    squares_in,
    gate_buf,
    up_buf,
    down_buf,
    part,
    part_in,
    hidden,
    buf_a,
    recv_a,
    buf_b,
    recv_b,
    g_sem,
    u_sem,
    d_sem,
    qs,
    qr,
    ps,
    pr,
    hs,
    hr,
    sa,
    ra,
    sb,
    rb,
):
    c, s, h = lax.axis_index("ctx"), lax.axis_index("smp"), lax.axis_index("head")
    steps = part.shape[0]
    slots = gate_buf.shape[0]
    tiles = down_buf.shape[0]
    width = state_ref.shape[3]
    all_rows = state_ref.shape[0] * 2 * state_ref.shape[2]
    smp_rows = all_rows // n_smp

    def weight_copies(t):
        slot = lax.rem(t, slots)
        return (
            pltpu.make_async_copy(
                gate_ref.at[:, columns(t, UNITS)], gate_buf.at[slot], g_sem.at[slot]
            ),
            pltpu.make_async_copy(up_ref.at[:, columns(t, UNITS)], up_buf.at[slot], u_sem.at[slot]),
        )

    def down_copy(t):
        return pltpu.make_async_copy(down_ref.at[:, columns(t, TILE)], down_buf.at[t], d_sem.at[t])

    @pl.loop(0, min(slots, steps))
    def _(t):
        for copy in weight_copies(t):
            copy.start()

    greet(n, n_smp, c, s, h)

    for block in range(n):
        wide = state_ref[block].reshape(-1, width).astype(jnp.float32)
        rows = slice(block * wide.shape[0], (block + 1) * wide.shape[0])
        scaled[rows] = (wide * gain_ref[...]).astype(jnp.bfloat16)
        sums = jnp.sum(wide * wide, axis=1, keepdims=True)
        squares[rows] = jnp.broadcast_to(sums, (wide.shape[0], 128))

    def smp_rows_of(p):
        return pl.ds(pl.multiple_of(p * smp_rows, smp_rows), smp_rows)

    def square_copy(k):
        p = lax.rem(s + k, n_smp)
        return remote(
            squares.at[smp_rows_of(p)], squares_in.at[k - 1], qs.at[k - 1], qr.at[k - 1], {"smp": p}
        )

    for k in range(1, n_smp):
        square_copy(k).start()

    def part_copy(t, k):
        p = lax.rem(s + k, n_smp)
        return remote(
            part.at[t, smp_rows_of(p)],
            part_in.at[t, k - 1],
            ps.at[t, k - 1],
            pr.at[t, k - 1],
            {"smp": p},
        )

    def hidden_copy(t, k):
        block = hidden.at[smp_rows_of(s), columns(t, UNITS)]
        return remote(
            block, block, hs.at[t, k - 1], hr.at[t, k - 1], {"smp": lax.rem(s + k, n_smp)}
        )

    def act(t):
        both = part[t, smp_rows_of(s)].astype(jnp.float32)
        for k in range(1, n_smp):
            part_copy(t, k).wait()
            both = both + part_in[t, k - 1].astype(jnp.float32)
        total = squares[smp_rows_of(s)]
        for k in range(1, n_smp):
            total = total + squares_in[k - 1]
        factor = lax.rsqrt(total / (width * n_smp) + EPSILON)[:, :1]
        gate = factor * both[:, :UNITS]
        up = factor * both[:, UNITS:]
        value = gate / (1.0 + jnp.exp(-gate)) * up
        hidden[smp_rows_of(s), columns(t, UNITS)] = value.astype(jnp.bfloat16)
        for k in range(1, n_smp):
            hidden_copy(t, k).start()

    lag = min(2, steps)

    @pl.loop(0, steps)
    def _(t):
        for copy in weight_copies(t):
            copy.wait()
        slot = lax.rem(t, slots)
        part[t, :, :UNITS] = jnp.dot(
            scaled[...], gate_buf[slot], preferred_element_type=jnp.float32
        ).astype(jnp.bfloat16)
        part[t, :, UNITS:] = jnp.dot(
            scaled[...], up_buf[slot], preferred_element_type=jnp.float32
        ).astype(jnp.bfloat16)
        for k in range(1, n_smp):
            part_copy(t, k).start()

        @pl.when(t + slots < steps)
        def _():
            for copy in weight_copies(t + slots):
                copy.start()

        @pl.when(t < tiles)
        def _():
            down_copy(t).start()

        @pl.when(t == lag)
        def _():
            for k in range(1, n_smp):
                square_copy(k).wait()

        @pl.when(t >= lag)
        def _():
            act(t - lag)

    if steps <= lag:
        for k in range(1, n_smp):
            square_copy(k).wait()

    for t in range(steps, tiles):
        down_copy(t).start()

    @pl.loop(steps - lag, steps)
    def _(t):
        act(t)

    @pl.loop(0, steps)
    def _(t):
        for k in range(1, n_smp):
            hidden_copy(t, k).wait()

    scatter = Scatter(n, c, h, buf_a, recv_a, buf_b, recv_b, sa, ra, sb, rb)

    @pl.loop(0, tiles)
    def _(t):
        down_copy(t).wait()
        scatter.give(t, jnp.dot(hidden[...], down_buf[t], preferred_element_type=jnp.float32))

        @pl.when(t >= 1)
        def _():
            scatter.middle(t - 1)

    scatter.middle(tiles - 1)

    @pl.loop(0, tiles)
    def _(t):
        own = scatter.finish(t) + state_ref[c, h, :, columns(t, TILE)].astype(jnp.float32)
        mixed_ref[:, columns(t, TILE)] = own.astype(jnp.bfloat16)


def feed_forward(n, n_smp, state, gain, gate, up, down):
    _, _, rows, width = state.shape
    all_rows = n * 2 * rows
    smp_rows = all_rows // n_smp
    units = gate.shape[1]
    steps, tiles = units // UNITS, width // TILE
    slots = min(SLOTS, steps)
    vmem = pl.BlockSpec(memory_space=pltpu.VMEM)
    hbm = pl.BlockSpec(memory_space=pl.ANY)
    dma = pltpu.SemaphoreType.DMA
    bf16 = jnp.bfloat16
    return pl.pallas_call(
        functools.partial(ffn_kernel, n, n_smp),
        out_shape=jax.ShapeDtypeStruct((rows, width), bf16),
        in_specs=[vmem, vmem, hbm, hbm, hbm],
        out_specs=vmem,
        scratch_shapes=[
            pltpu.VMEM((all_rows, width), bf16),
            pltpu.VMEM((all_rows, 128), jnp.float32),
            pltpu.VMEM((n_smp - 1, smp_rows, 128), jnp.float32),
            pltpu.VMEM((slots, width, UNITS), bf16),
            pltpu.VMEM((slots, width, UNITS), bf16),
            pltpu.VMEM((tiles, units, TILE), bf16),
            pltpu.VMEM((steps, all_rows, 2 * UNITS), bf16),
            pltpu.VMEM((steps, n_smp - 1, smp_rows, 2 * UNITS), bf16),
            pltpu.VMEM((all_rows, units), bf16),
            pltpu.VMEM((tiles, 2, n, rows, TILE), bf16),
            pltpu.VMEM((tiles, n, rows, TILE), bf16),
            pltpu.VMEM((tiles, n, rows, TILE), bf16),
            pltpu.VMEM((tiles, n - 1, rows, TILE), bf16),
            dma((slots,)),
            dma((slots,)),
            dma((tiles,)),
            dma((n_smp - 1,)),
            dma((n_smp - 1,)),
            dma((steps, n_smp - 1)),
            dma((steps, n_smp - 1)),
            dma((steps, n_smp - 1)),
            dma((steps, n_smp - 1)),
            dma((tiles,)),
            dma((tiles,)),
            dma((tiles, n - 1)),
            dma((tiles, n - 1)),
        ],
        compiler_params=pltpu.CompilerParams(
            collective_id=1, has_side_effects=True, vmem_limit_bytes=VMEM_BYTES
        ),
    )(state, gain, gate, up, down)


def on_device(
    queries,
    prefix_cache,
    suffix_cache,
    suffix_length,
    cache_sample,
    residual,
    w_out,
    norm_gain,
    gate_matrix,
    w_up,
    w_down,
):
    group_rows = queries.shape[0]
    key_value_heads_here = prefix_cache.shape[3] // HD
    queries_per_key_value = QUERY_HEADS // KEY_VALUE_HEADS
    heads_local = key_value_heads_here * queries_per_key_value
    score_scale = HD ** (-0.5)
    queries_split = queries.reshape(group_rows, key_value_heads_here, queries_per_key_value, HD)
    prefix_keys = prefix_cache[0].reshape(-1, key_value_heads_here, HD)
    prefix_values = prefix_cache[1].reshape(-1, key_value_heads_here, HD)
    scores = (
        jnp.einsum("sjgd,pjd->jsgp", queries_split, prefix_keys, preferred_element_type=jnp.float32)
        * score_scale
    )
    highest = jnp.max(scores, axis=3)
    weights = jnp.exp(scores - highest[..., None])
    totals = jnp.sum(weights, axis=3)
    summed = jnp.einsum(
        "jsgp,pjd->sjgd",
        weights.astype(jnp.bfloat16),
        prefix_values,
        preferred_element_type=jnp.float32,
    )
    prefix_out = (summed / jnp.transpose(totals, (1, 0, 2))[..., None]).astype(jnp.bfloat16)
    prefix_lse = jnp.transpose(highest + jnp.log(totals), (1, 0, 2))
    rows_here = suffix_cache.shape[1]
    flat_index = lax.axis_index("ctx") * lax.axis_size("smp") + lax.axis_index("smp")
    row_ids = lax.dynamic_slice_in_dim(cache_sample, flat_index * rows_here, rows_here, 0)
    local_ids = row_ids % group_rows
    row_queries = jnp.take(queries_split, local_ids, axis=0)
    row_lengths = jnp.take(suffix_length, local_ids, axis=0)
    suffix_out, suffix_lse = suffix_piece(
        row_queries, suffix_cache, row_lengths, key_value_heads_here, score_scale
    )
    onehot = (local_ids[None, :] == jnp.arange(group_rows, dtype=jnp.int32)[:, None]).astype(
        jnp.float32
    )
    present = jnp.sum(onehot, axis=1)[:, None]
    placed_out = jnp.dot(
        onehot,
        suffix_out.reshape(rows_here, -1).astype(jnp.float32),
        precision=lax.Precision.HIGHEST,
    )
    placed_lse = jnp.dot(
        onehot, suffix_lse.reshape(rows_here, heads_local), precision=lax.Precision.HIGHEST
    )
    own_lse = prefix_lse.reshape(group_rows, heads_local)
    other_lse = jnp.where(present > 0, placed_lse, own_lse)
    top = jnp.maximum(own_lse, other_lse)
    own_weight = jnp.exp(own_lse - top)
    other_weight = present * jnp.exp(other_lse - top)
    both_weight = own_weight + other_weight
    own_values = prefix_out.reshape(group_rows, heads_local, HD).astype(jnp.float32)
    other_values = placed_out.reshape(group_rows, heads_local, HD)
    local_out = (
        own_weight[..., None] * own_values + other_weight[..., None] * other_values
    ) / both_weight[..., None]
    local_lse = top + jnp.log(both_weight)
    n, n_smp = lax.axis_size("ctx"), lax.axis_size("smp")
    pieces = local_out.astype(jnp.bfloat16).reshape(group_rows, n, -1).transpose(1, 0, 2)
    piece_lse = local_lse.reshape(group_rows, n, -1).transpose(1, 0, 2)
    state = project(n, n_smp, pieces, piece_lse, w_out[0], residual)
    return feed_forward(n, n_smp, state, norm_gain[None, :], gate_matrix, w_up, w_down)


def solution(mesh):
    in_specs = (
        P(("group", "smp"), "head", None),
        P(None, ("group", "ctx"), "head", None),
        P(None, ("group", "ctx", "smp"), None, "head", None),
        P(("group", "smp")),
        P("group"),
        P(("group", "ctx", "head"), "smp"),
        P("head", "ctx", "smp"),
        P("smp"),
        P("smp", ("ctx", "head")),
        P("smp", ("ctx", "head")),
        P(("ctx", "head"), "smp"),
    )
    out_specs = P(("group", "ctx", "head"), "smp")
    return jax.shard_map(
        on_device, mesh=mesh, in_specs=in_specs, out_specs=out_specs, check_vma=False
    )
```

```python
import functools

import jax
import jax.numpy as jnp
from jax import lax
from jax.experimental import pallas as pl
from jax.experimental.pallas import tpu as pltpu
from jax.sharding import PartitionSpec as P

D = 8192
QUERY_HEADS = 64
KEY_VALUE_HEADS = 8
HD = 128


EPSILON = 1e-05


def suffix_kernel(lengths_ref, queries_ref, cache_ref, out_ref, lse_ref):
    block, heads, _ = queries_ref.shape
    positions_here, width = cache_ref.shape[2:]
    per_key = heads // (width // HD)
    first = pl.program_id(0) * block
    same = (
        lax.broadcasted_iota(jnp.int32, (heads, width), 0) // per_key
        == lax.broadcasted_iota(jnp.int32, (heads, width), 1) // HD
    )
    positions = lax.broadcasted_iota(jnp.int32, (heads, positions_here), 1)
    for r in range(block):
        q = queries_ref[r].astype(jnp.float32)
        spread = jnp.concatenate([q] * (width // HD), axis=1)
        spread = jnp.where(same, spread, 0.0).astype(jnp.bfloat16)
        scores = lax.dot_general(
            spread, cache_ref[0, r], (((1,), (1,)), ((), ())), preferred_element_type=jnp.float32
        )
        scores = jnp.where(positions < lengths_ref[first + r], scores * HD ** (-0.5), -jnp.inf)
        high = jnp.max(scores, axis=1, keepdims=True)
        weights = jnp.exp(scores - high)
        total = jnp.sum(weights, axis=1, keepdims=True)
        summed = jnp.dot(
            weights.astype(jnp.bfloat16), cache_ref[1, r], preferred_element_type=jnp.float32
        )
        own = jnp.concatenate(
            [
                summed[j * per_key : (j + 1) * per_key, j * HD : (j + 1) * HD]
                for j in range(width // HD)
            ],
            axis=0,
        )
        out_ref[r] = (own / total).astype(jnp.bfloat16)
        lse_ref[r] = high + jnp.log(total)


def suffix_piece(row_queries, suffix_cache, row_lengths):
    rows, heads, _ = row_queries.shape
    block = min(8, rows)
    _, _, positions_here, width = suffix_cache.shape
    return pl.pallas_call(
        suffix_kernel,
        grid=(rows // block,),
        out_shape=(
            jax.ShapeDtypeStruct((rows, heads, HD), jnp.bfloat16),
            jax.ShapeDtypeStruct((rows, heads, 1), jnp.float32),
        ),
        in_specs=[
            pl.BlockSpec(memory_space=pltpu.SMEM),
            pl.BlockSpec((block, heads, HD), lambda i: (i, 0, 0)),
            pl.BlockSpec((2, block, positions_here, width), lambda i: (0, i, 0, 0)),
        ],
        out_specs=(
            pl.BlockSpec((block, heads, HD), lambda i: (i, 0, 0)),
            pl.BlockSpec((block, heads, 1), lambda i: (i, 0, 0)),
        ),
        compiler_params=pltpu.CompilerParams(vmem_limit_bytes=32 * 1024 * 1024),
    )(row_lengths, row_queries, suffix_cache)


MESH = pl.DeviceIdType.MESH
TILE = 512
VMEM_BYTES = 62 * 1024 * 1024


def remote(src, dst, send_sem, recv_sem, where):
    return pltpu.make_async_remote_copy(
        src_ref=src,
        dst_ref=dst,
        send_sem=send_sem,
        recv_sem=recv_sem,
        device_id=where,
        device_id_type=MESH,
    )


def greet(n, n_smp, c, s, h):
    barrier = pltpu.get_barrier_semaphore()
    for k in range(1, n):
        pl.semaphore_signal(barrier, inc=1, device_id={"ctx": lax.rem(c + k, n)}, device_id_type=MESH)
    for k in range(1, n_smp):
        pl.semaphore_signal(
            barrier, inc=1, device_id={"smp": lax.rem(s + k, n_smp)}, device_id_type=MESH
        )
    pl.semaphore_signal(barrier, inc=1, device_id={"head": 1 - h}, device_id_type=MESH)
    pl.semaphore_wait(barrier, (n - 1) + (n_smp - 1) + 1)


class Scatter:
    def __init__(self, n, c, h, buf_a, recv_a, buf_b, recv_b, sa, ra, sb, rb):
        self.n, self.c, self.h = n, c, h
        self.buf_a, self.recv_a, self.buf_b, self.recv_b = buf_a, recv_a, buf_b, recv_b
        self.sa, self.ra, self.sb, self.rb = sa, ra, sb, rb

    def pair_copy(self, t):
        return remote(
            self.buf_a.at[t, 1 - self.h],
            self.recv_a.at[t],
            self.sa.at[t],
            self.ra.at[t],
            {"head": 1 - self.h},
        )

    def row_copy(self, t, k):
        d = lax.rem(self.c + k, self.n)
        return remote(
            self.buf_b.at[t, d],
            self.recv_b.at[t, k - 1],
            self.sb.at[t, k - 1],
            self.rb.at[t, k - 1],
            {"ctx": d},
        )

    def give(self, t, value):
        _, _, n, rows, width = self.buf_a.shape
        parts = value.reshape(n, 2, rows, width).astype(jnp.bfloat16)
        self.buf_a[t, 0] = parts[:, 0]
        self.buf_a[t, 1] = parts[:, 1]
        self.pair_copy(t).start()

    def middle(self, t):
        self.pair_copy(t).wait()
        both = self.buf_a[t, self.h].astype(jnp.float32) + self.recv_a[t].astype(jnp.float32)
        self.buf_b[t] = both.astype(jnp.bfloat16)
        for k in range(1, self.n):
            self.row_copy(t, k).start()

    def finish(self, t):
        total = self.buf_b[t, self.c].astype(jnp.float32)
        for k in range(1, self.n):
            self.row_copy(t, k).wait()
            total = total + self.recv_b[t, k - 1].astype(jnp.float32)
        return total


def columns(t, width):
    return pl.ds(pl.multiple_of(t * width, width), width)


def proj_kernel(
    n,
    n_smp,
    q_ref,
    kv_ref,
    suf_ref,
    suf_lse_ref,
    w_ref,
    res_ref,
    state_ref,
    out_mine,
    lse_mine,
    out_in,
    lse_in,
    attn,
    w_buf,
    buf_a,
    recv_a,
    buf_b,
    recv_b,
    w_sem,
    os,
    orr,
    ls,
    lr,
    xs,
    xr,
    sa,
    ra,
    sb,
    rb,
    gs,
    gr,
    fs,
    fr,
):
    c, s, h = lax.axis_index("ctx"), lax.axis_index("smp"), lax.axis_index("head")
    tiles = w_buf.shape[0]
    keys, samples, per_key = suf_lse_ref.shape
    per_dest = out_mine.shape[2] // HD
    dests = per_key // per_dest
    together = 4

    greet(n, n_smp, c, s, h)

    def piece_copies(at, d):
        return (
            remote(out_mine.at[d], out_in.at[at], os.at[d], orr.at[at], {"ctx": d}),
            remote(lse_mine.at[d], lse_in.at[at], ls.at[d], lr.at[at], {"ctx": d}),
        )

    def w_copy(t):
        return pltpu.make_async_copy(w_ref.at[:, columns(t, TILE)], w_buf.at[t], w_sem.at[t])

    @pl.loop(0, tiles)
    def _(t):
        w_copy(t).start()

    lanes_at = lax.broadcasted_iota(jnp.int32, (samples, 128), 1)

    @pl.loop(0, keys)
    def _(i):
        j = lax.rem(lax.div(c, dests) + 1 + i, keys)
        key = kv_ref[0, :, columns(j, HD)]
        value = kv_ref[1, :, columns(j, HD)]
        own = q_ref[:, columns(j, per_key * HD)]
        placed = suf_ref[:, columns(j, per_key * HD)]
        placed_lse = suf_lse_ref[j]
        tables = [jnp.zeros((samples, 128), jnp.float32) for _ in range(dests)]
        for g0 in range(0, per_key, together):
            rows = jnp.concatenate(
                [own[:, g * HD : (g + 1) * HD] for g in range(g0, g0 + together)], axis=0
            )
            scores = lax.dot_general(
                rows, key, (((1,), (1,)), ((), ())), preferred_element_type=jnp.float32
            ) * HD ** (-0.5)
            high = jnp.max(scores, axis=1, keepdims=True)
            weights = jnp.exp(scores - high)
            total = jnp.sum(weights, axis=1, keepdims=True)
            summed = (
                jnp.dot(weights.astype(jnp.bfloat16), value, preferred_element_type=jnp.float32)
                / total
            )
            lse = high + jnp.log(total)
            for g in range(g0, g0 + together):
                part = slice((g - g0) * samples, (g - g0 + 1) * samples)
                own_lse, other_lse = lse[part], placed_lse[:, g : g + 1]
                top = jnp.maximum(own_lse, other_lse)
                own_weight = jnp.exp(own_lse - top)
                other_weight = jnp.exp(other_lse - top)
                both = own_weight + other_weight
                merged = (
                    own_weight * summed[part]
                    + other_weight * placed[:, g * HD : (g + 1) * HD].astype(jnp.float32)
                ) / both
                at = g % per_dest
                out_mine[j * dests + g // per_dest, :, at * HD : (at + 1) * HD] = merged.astype(
                    jnp.bfloat16
                )
                q = g // per_dest
                tables[q] = jnp.where(lanes_at == at, top + jnp.log(both), tables[q])
        for q in range(dests):
            d = j * dests + q
            lse_mine[d] = tables[q].T[:8]

            @pl.when(d != c)
            def _():
                for copy in piece_copies(c, d):
                    copy.start()

    for k in range(1, n):
        d = lax.rem(c + k, n)
        for copy in piece_copies(d, d):
            copy.wait_recv()
    for k in range(1, n):
        d = lax.rem(c + k, n)
        for copy in piece_copies(c, d):
            copy.wait_send()

    lses = [lse_mine[c]] + [lse_in[lax.rem(c + k, n)] for k in range(1, n)]
    peak = functools.reduce(jnp.maximum, lses)
    scales = [jnp.exp(value - peak) for value in lses]
    denom = functools.reduce(jnp.add, scales)
    blank = jnp.zeros((120, samples), jnp.float32)
    scales = [jnp.concatenate([value / denom, blank], axis=0).T for value in scales]
    for j in range(per_dest):
        lanes = slice(j * HD, (j + 1) * HD)
        total = scales[0][:, j : j + 1] * out_mine[c, :, lanes].astype(jnp.float32)
        for k in range(1, n):
            piece = out_in[lax.rem(c + k, n), :, lanes].astype(jnp.float32)
            total = total + scales[k][:, j : j + 1] * piece
        attn[s, :, lanes] = total.astype(jnp.bfloat16)

    def attn_copy(k):
        return remote(
            attn.at[s], attn.at[s], xs.at[k - 1], xr.at[k - 1], {"smp": lax.rem(s + k, n_smp)}
        )

    for k in range(1, n_smp):
        attn_copy(k).start()
    for k in range(1, n_smp):
        attn_copy(k).wait()

    scatter = Scatter(n, c, h, buf_a, recv_a, buf_b, recv_b, sa, ra, sb, rb)

    @pl.loop(0, tiles)
    def _(t):
        w_copy(t).wait()
        rows = attn[...].reshape(-1, attn.shape[2])
        scatter.give(t, jnp.dot(rows, w_buf[t], preferred_element_type=jnp.float32))

        @pl.when(t >= 1)
        def _():
            scatter.middle(t - 1)

    scatter.middle(tiles - 1)

    def gather_copy(t, k):
        block = state_ref.at[c, h, :, columns(t, TILE)]
        return remote(
            block, block, gs.at[t, k - 1], gr.at[t, k - 1], {"ctx": lax.rem(c + k, n)}
        )

    def pass_copy(t, k):
        block = state_ref.at[lax.rem(c + n - k, n), h, :, columns(t, TILE)]
        return remote(block, block, fs.at[t, k], fr.at[t, k], {"head": 1 - h})

    @pl.loop(0, tiles)
    def _(t):
        own = scatter.finish(t) + res_ref[:, columns(t, TILE)].astype(jnp.float32)
        state_ref[c, h, :, columns(t, TILE)] = own.astype(jnp.bfloat16)
        for k in range(1, n):
            gather_copy(t, k).start()
        pass_copy(t, 0).start()

    @pl.loop(0, tiles)
    def _(t):
        for k in range(1, n):
            gather_copy(t, k).wait()
            pass_copy(t, k).start()

    @pl.loop(0, tiles)
    def _(t):
        for k in range(n):
            pass_copy(t, k).wait()


def project(n, n_smp, queries, prefix_cache, suffix_out, suffix_lse, w, residual):
    keys, samples, per_key = suffix_lse.shape
    features = queries.shape[1] // n
    rows, width = residual.shape
    tiles = width // TILE
    vmem = pl.BlockSpec(memory_space=pltpu.VMEM)
    dma = pltpu.SemaphoreType.DMA
    bf16 = jnp.bfloat16
    return pl.pallas_call(
        functools.partial(proj_kernel, n, n_smp),
        out_shape=jax.ShapeDtypeStruct((n, 2, rows, width), bf16),
        in_specs=[vmem, vmem, vmem, vmem, pl.BlockSpec(memory_space=pl.ANY), vmem],
        out_specs=vmem,
        scratch_shapes=[
            pltpu.VMEM((n, samples, features), bf16),
            pltpu.VMEM((n, 8, samples), jnp.float32),
            pltpu.VMEM((n, samples, features), bf16),
            pltpu.VMEM((n, 8, samples), jnp.float32),
            pltpu.VMEM((n_smp, samples, features), bf16),
            pltpu.VMEM((tiles, w.shape[0], TILE), bf16),
            pltpu.VMEM((tiles, 2, n, rows, TILE), bf16),
            pltpu.VMEM((tiles, n, rows, TILE), bf16),
            pltpu.VMEM((tiles, n, rows, TILE), bf16),
            pltpu.VMEM((tiles, n - 1, rows, TILE), bf16),
            dma((tiles,)),
            dma((n,)),
            dma((n,)),
            dma((n,)),
            dma((n,)),
            dma((n_smp - 1,)),
            dma((n_smp - 1,)),
            dma((tiles,)),
            dma((tiles,)),
            dma((tiles, n - 1)),
            dma((tiles, n - 1)),
            dma((tiles, n - 1)),
            dma((tiles, n - 1)),
            dma((tiles, n)),
            dma((tiles, n)),
        ],
        compiler_params=pltpu.CompilerParams(
            collective_id=0, has_side_effects=True, vmem_limit_bytes=VMEM_BYTES
        ),
    )(queries, prefix_cache, suffix_out, suffix_lse, w, residual)


UNITS = 256
SLOTS = 4


def ffn_kernel(
    n,
    n_smp,
    state_ref,
    gain_ref,
    gate_ref,
    up_ref,
    down_ref,
    mixed_ref,
    scaled,
    squares,
    squares_in,
    gate_buf,
    up_buf,
    down_buf,
    part,
    part_in,
    hidden,
    buf_a,
    recv_a,
    buf_b,
    recv_b,
    g_sem,
    u_sem,
    d_sem,
    qs,
    qr,
    ps,
    pr,
    hs,
    hr,
    sa,
    ra,
    sb,
    rb,
):
    c, s, h = lax.axis_index("ctx"), lax.axis_index("smp"), lax.axis_index("head")
    steps = part.shape[0]
    slots = gate_buf.shape[0]
    tiles = down_buf.shape[0]
    width = state_ref.shape[3]
    all_rows = state_ref.shape[0] * 2 * state_ref.shape[2]
    smp_rows = all_rows // n_smp

    def weight_copies(t):
        slot = lax.rem(t, slots)
        return (
            pltpu.make_async_copy(
                gate_ref.at[:, columns(t, UNITS)], gate_buf.at[slot], g_sem.at[slot]
            ),
            pltpu.make_async_copy(up_ref.at[:, columns(t, UNITS)], up_buf.at[slot], u_sem.at[slot]),
        )

    def down_copy(t):
        return pltpu.make_async_copy(down_ref.at[:, columns(t, TILE)], down_buf.at[t], d_sem.at[t])

    @pl.loop(0, min(slots, steps))
    def _(t):
        for copy in weight_copies(t):
            copy.start()

    greet(n, n_smp, c, s, h)

    for block in range(n):
        wide = state_ref[block].reshape(-1, width).astype(jnp.float32)
        rows = slice(block * wide.shape[0], (block + 1) * wide.shape[0])
        scaled[rows] = (wide * gain_ref[...]).astype(jnp.bfloat16)
        sums = jnp.sum(wide * wide, axis=1, keepdims=True)
        squares[rows] = jnp.broadcast_to(sums, (wide.shape[0], 128))

    def smp_rows_of(p):
        return pl.ds(pl.multiple_of(p * smp_rows, smp_rows), smp_rows)

    def square_copy(k):
        p = lax.rem(s + k, n_smp)
        return remote(
            squares.at[smp_rows_of(p)], squares_in.at[k - 1], qs.at[k - 1], qr.at[k - 1], {"smp": p}
        )

    for k in range(1, n_smp):
        square_copy(k).start()

    def part_copy(t, k):
        p = lax.rem(s + k, n_smp)
        return remote(
            part.at[t, smp_rows_of(p)],
            part_in.at[t, k - 1],
            ps.at[t, k - 1],
            pr.at[t, k - 1],
            {"smp": p},
        )

    def hidden_copy(t, k):
        block = hidden.at[smp_rows_of(s), columns(t, UNITS)]
        return remote(
            block, block, hs.at[t, k - 1], hr.at[t, k - 1], {"smp": lax.rem(s + k, n_smp)}
        )

    def act(t):
        both = part[t, smp_rows_of(s)].astype(jnp.float32)
        for k in range(1, n_smp):
            part_copy(t, k).wait()
            both = both + part_in[t, k - 1].astype(jnp.float32)
        total = squares[smp_rows_of(s)]
        for k in range(1, n_smp):
            total = total + squares_in[k - 1]
        factor = lax.rsqrt(total / (width * n_smp) + EPSILON)[:, :1]
        gate = factor * both[:, :UNITS]
        up = factor * both[:, UNITS:]
        value = gate / (1.0 + jnp.exp(-gate)) * up
        hidden[smp_rows_of(s), columns(t, UNITS)] = value.astype(jnp.bfloat16)
        for k in range(1, n_smp):
            hidden_copy(t, k).start()

    lag = min(2, steps)

    @pl.loop(0, steps)
    def _(t):
        for copy in weight_copies(t):
            copy.wait()
        slot = lax.rem(t, slots)
        part[t, :, :UNITS] = jnp.dot(
            scaled[...], gate_buf[slot], preferred_element_type=jnp.float32
        ).astype(jnp.bfloat16)
        part[t, :, UNITS:] = jnp.dot(
            scaled[...], up_buf[slot], preferred_element_type=jnp.float32
        ).astype(jnp.bfloat16)
        for k in range(1, n_smp):
            part_copy(t, k).start()

        @pl.when(t + slots < steps)
        def _():
            for copy in weight_copies(t + slots):
                copy.start()

        @pl.when(t < tiles)
        def _():
            down_copy(t).start()

        @pl.when(t == lag)
        def _():
            for k in range(1, n_smp):
                square_copy(k).wait()

        @pl.when(t >= lag)
        def _():
            act(t - lag)

    if steps <= lag:
        for k in range(1, n_smp):
            square_copy(k).wait()

    for t in range(steps, tiles):
        down_copy(t).start()

    @pl.loop(steps - lag, steps)
    def _(t):
        act(t)

    @pl.loop(0, steps)
    def _(t):
        for k in range(1, n_smp):
            hidden_copy(t, k).wait()

    scatter = Scatter(n, c, h, buf_a, recv_a, buf_b, recv_b, sa, ra, sb, rb)

    @pl.loop(0, tiles)
    def _(t):
        down_copy(t).wait()
        scatter.give(t, jnp.dot(hidden[...], down_buf[t], preferred_element_type=jnp.float32))

        @pl.when(t >= 1)
        def _():
            scatter.middle(t - 1)

    scatter.middle(tiles - 1)

    @pl.loop(0, tiles)
    def _(t):
        own = scatter.finish(t) + state_ref[c, h, :, columns(t, TILE)].astype(jnp.float32)
        mixed_ref[:, columns(t, TILE)] = own.astype(jnp.bfloat16)


def feed_forward(n, n_smp, state, gain, gate, up, down):
    _, _, rows, width = state.shape
    all_rows = n * 2 * rows
    smp_rows = all_rows // n_smp
    units = gate.shape[1]
    steps, tiles = units // UNITS, width // TILE
    slots = min(SLOTS, steps)
    vmem = pl.BlockSpec(memory_space=pltpu.VMEM)
    hbm = pl.BlockSpec(memory_space=pl.ANY)
    dma = pltpu.SemaphoreType.DMA
    bf16 = jnp.bfloat16
    return pl.pallas_call(
        functools.partial(ffn_kernel, n, n_smp),
        out_shape=jax.ShapeDtypeStruct((rows, width), bf16),
        in_specs=[vmem, vmem, hbm, hbm, hbm],
        out_specs=vmem,
        scratch_shapes=[
            pltpu.VMEM((all_rows, width), bf16),
            pltpu.VMEM((all_rows, 128), jnp.float32),
            pltpu.VMEM((n_smp - 1, smp_rows, 128), jnp.float32),
            pltpu.VMEM((slots, width, UNITS), bf16),
            pltpu.VMEM((slots, width, UNITS), bf16),
            pltpu.VMEM((tiles, units, TILE), bf16),
            pltpu.VMEM((steps, all_rows, 2 * UNITS), bf16),
            pltpu.VMEM((steps, n_smp - 1, smp_rows, 2 * UNITS), bf16),
            pltpu.VMEM((all_rows, units), bf16),
            pltpu.VMEM((tiles, 2, n, rows, TILE), bf16),
            pltpu.VMEM((tiles, n, rows, TILE), bf16),
            pltpu.VMEM((tiles, n, rows, TILE), bf16),
            pltpu.VMEM((tiles, n - 1, rows, TILE), bf16),
            dma((slots,)),
            dma((slots,)),
            dma((tiles,)),
            dma((n_smp - 1,)),
            dma((n_smp - 1,)),
            dma((steps, n_smp - 1)),
            dma((steps, n_smp - 1)),
            dma((steps, n_smp - 1)),
            dma((steps, n_smp - 1)),
            dma((tiles,)),
            dma((tiles,)),
            dma((tiles, n - 1)),
            dma((tiles, n - 1)),
        ],
        compiler_params=pltpu.CompilerParams(
            collective_id=1, has_side_effects=True, vmem_limit_bytes=VMEM_BYTES
        ),
    )(state, gain, gate, up, down)


def on_device(
    queries,
    prefix_cache,
    suffix_cache,
    suffix_length,
    cache_sample,
    residual,
    w_out,
    norm_gain,
    gate_matrix,
    w_up,
    w_down,
):
    group_rows = queries.shape[0]
    keys_here = prefix_cache.shape[3] // HD
    heads_local = queries.shape[2] // HD
    n, n_smp = lax.axis_size("ctx"), lax.axis_size("smp")
    own_queries = queries[:, 0]
    rows_here = suffix_cache.shape[1]
    flat_index = lax.axis_index("ctx") * n_smp + lax.axis_index("smp")
    row_ids = lax.dynamic_slice_in_dim(cache_sample, flat_index * rows_here, rows_here, 0)
    local_ids = row_ids % group_rows
    row_queries = jnp.take(own_queries, local_ids, axis=0).reshape(rows_here, heads_local, HD)
    row_lengths = jnp.take(suffix_length, local_ids, axis=0)
    suffix_out, suffix_lse = suffix_piece(row_queries, suffix_cache[:, :, :, 0], row_lengths)
    chosen = local_ids[None, :] == jnp.arange(group_rows, dtype=jnp.int32)[:, None]
    placed_out = jnp.dot(
        chosen.astype(jnp.bfloat16),
        suffix_out.reshape(rows_here, -1),
        preferred_element_type=jnp.float32,
    ).astype(jnp.bfloat16)
    placed_lse = jnp.dot(
        chosen.astype(jnp.float32), suffix_lse[:, :, 0], precision=lax.Precision.HIGHEST
    )
    placed_lse = jnp.where(jnp.any(chosen, axis=1)[:, None], placed_lse, -1e30)
    placed_lse = placed_lse.reshape(group_rows, keys_here, -1).transpose(1, 0, 2)
    state = project(
        n,
        n_smp,
        own_queries,
        prefix_cache[:, :, 0],
        placed_out,
        placed_lse,
        w_out[0],
        residual,
    )
    return feed_forward(n, n_smp, state, norm_gain[None, :], gate_matrix, w_up, w_down)


def solution(mesh):
    in_specs = (
        P(("group", "smp"), "head", None),
        P(None, ("group", "ctx"), "head", None),
        P(None, ("group", "ctx", "smp"), None, "head", None),
        P(("group", "smp")),
        P("group"),
        P(("group", "ctx", "head"), "smp"),
        P("head", "ctx", "smp"),
        P("smp"),
        P("smp", ("ctx", "head")),
        P("smp", ("ctx", "head")),
        P(("ctx", "head"), "smp"),
    )
    out_specs = P(("group", "ctx", "head"), "smp")
    return jax.shard_map(
        on_device, mesh=mesh, in_specs=in_specs, out_specs=out_specs, check_vma=False
    )
```

```python
import functools

import jax
import jax.numpy as jnp
from jax import lax
from jax.experimental import pallas as pl
from jax.experimental.pallas import tpu as pltpu
from jax.sharding import PartitionSpec as P

D = 8192
QUERY_HEADS = 64
KEY_VALUE_HEADS = 8
HD = 128


EPSILON = 1e-05


def suffix_kernel(lengths_ref, queries_ref, cache_ref, out_ref, lse_ref):
    block, heads, _ = queries_ref.shape
    positions_here, width = cache_ref.shape[2:]
    per_key = heads // (width // HD)
    first = pl.program_id(0) * block
    same = (
        lax.broadcasted_iota(jnp.int32, (heads, width), 0) // per_key
        == lax.broadcasted_iota(jnp.int32, (heads, width), 1) // HD
    )
    positions = lax.broadcasted_iota(jnp.int32, (heads, positions_here), 1)
    for r in range(block):
        q = queries_ref[r].astype(jnp.float32)
        spread = jnp.concatenate([q] * (width // HD), axis=1)
        spread = jnp.where(same, spread, 0.0).astype(jnp.bfloat16)
        scores = lax.dot_general(
            spread, cache_ref[0, r], (((1,), (1,)), ((), ())), preferred_element_type=jnp.float32
        )
        scores = jnp.where(positions < lengths_ref[first + r], scores * HD ** (-0.5), -jnp.inf)
        high = jnp.max(scores, axis=1, keepdims=True)
        weights = jnp.exp(scores - high)
        total = jnp.sum(weights, axis=1, keepdims=True)
        summed = jnp.dot(
            weights.astype(jnp.bfloat16), cache_ref[1, r], preferred_element_type=jnp.float32
        )
        own = jnp.concatenate(
            [
                summed[j * per_key : (j + 1) * per_key, j * HD : (j + 1) * HD]
                for j in range(width // HD)
            ],
            axis=0,
        )
        out_ref[r] = (own / total).astype(jnp.bfloat16)
        lse_ref[r] = high + jnp.log(total)


def suffix_piece(row_queries, suffix_cache, row_lengths):
    rows, heads, _ = row_queries.shape
    block = min(8, rows)
    _, _, positions_here, width = suffix_cache.shape
    return pl.pallas_call(
        suffix_kernel,
        grid=(rows // block,),
        out_shape=(
            jax.ShapeDtypeStruct((rows, heads, HD), jnp.bfloat16),
            jax.ShapeDtypeStruct((rows, heads, 1), jnp.float32),
        ),
        in_specs=[
            pl.BlockSpec(memory_space=pltpu.SMEM),
            pl.BlockSpec((block, heads, HD), lambda i: (i, 0, 0)),
            pl.BlockSpec((2, block, positions_here, width), lambda i: (0, i, 0, 0)),
        ],
        out_specs=(
            pl.BlockSpec((block, heads, HD), lambda i: (i, 0, 0)),
            pl.BlockSpec((block, heads, 1), lambda i: (i, 0, 0)),
        ),
        compiler_params=pltpu.CompilerParams(vmem_limit_bytes=32 * 1024 * 1024),
    )(row_lengths, row_queries, suffix_cache)


MESH = pl.DeviceIdType.MESH
TILE = 512
VMEM_BYTES = 62 * 1024 * 1024


def remote(src, dst, send_sem, recv_sem, where):
    return pltpu.make_async_remote_copy(
        src_ref=src,
        dst_ref=dst,
        send_sem=send_sem,
        recv_sem=recv_sem,
        device_id=where,
        device_id_type=MESH,
    )


def greet(n, n_smp, c, s, h):
    barrier = pltpu.get_barrier_semaphore()
    for k in range(1, n):
        pl.semaphore_signal(barrier, inc=1, device_id={"ctx": lax.rem(c + k, n)}, device_id_type=MESH)
    for k in range(1, n_smp):
        pl.semaphore_signal(
            barrier, inc=1, device_id={"smp": lax.rem(s + k, n_smp)}, device_id_type=MESH
        )
    pl.semaphore_signal(barrier, inc=1, device_id={"head": 1 - h}, device_id_type=MESH)
    pl.semaphore_wait(barrier, (n - 1) + (n_smp - 1) + 1)


class Line:
    def __init__(self, n, c, h, buf_a, recv_a, buf_b, from_left, from_right, sa, ra, ss, rl, rr):
        self.n, self.c, self.h = n, c, h
        self.buf_a, self.recv_a, self.buf_b = buf_a, recv_a, buf_b
        self.from_left, self.from_right = from_left, from_right
        self.sa, self.ra, self.ss, self.rl, self.rr = sa, ra, ss, rl, rr
        self.tiles = buf_a.shape[0]

        @pl.when(c == 0)
        def _():
            from_left[:, 0] = jnp.zeros(from_left.shape[:1] + from_left.shape[2:], from_left.dtype)

        @pl.when(c == n - 1)
        def _():
            from_right[:, n - 1] = jnp.zeros(
                from_right.shape[:1] + from_right.shape[2:], from_right.dtype
            )

    def pair_copy(self, t):
        return remote(
            self.buf_a.at[t, 1 - self.h],
            self.recv_a.at[t],
            self.sa.at[t],
            self.ra.at[t],
            {"head": 1 - self.h},
        )

    def to_right(self, t, d):
        return remote(
            self.buf_b.at[t, d],
            self.from_left.at[t, d],
            self.ss.at[t, d],
            self.rl.at[t, d],
            {"ctx": lax.rem(self.c + 1, self.n)},
        )

    def to_left(self, t, d):
        return remote(
            self.buf_b.at[t, d],
            self.from_right.at[t, d],
            self.ss.at[t, d],
            self.rr.at[t, d],
            {"ctx": lax.rem(self.c + self.n - 1, self.n)},
        )

    def give(self, t, value):
        _, _, n, rows, width = self.buf_a.shape
        parts = value.reshape(n, 2, rows, width).astype(jnp.bfloat16)
        self.buf_a[t, 0] = parts[:, 0]
        self.buf_a[t, 1] = parts[:, 1]
        self.pair_copy(t).start()

    def middle(self, t):
        self.pair_copy(t).wait()
        both = self.buf_a[t, self.h].astype(jnp.float32) + self.recv_a[t].astype(jnp.float32)
        self.buf_b[t] = both.astype(jnp.bfloat16)

    def hop(self, t, inside, d, copy_of, arrived, first):
        @pl.when(inside & (t >= 0) & (t < self.tiles))
        def _():
            @pl.when(jnp.logical_not(first))
            def _():
                copy_of(t, d).wait_recv()
                both = self.buf_b[t, d].astype(jnp.float32) + arrived[t, d].astype(jnp.float32)
                self.buf_b[t, d] = both.astype(jnp.bfloat16)

            copy_of(t, d).start()

    def step(self, i):
        n, c = self.n, self.c

        @pl.when((i >= 1) & (i <= self.tiles))
        def _():
            self.middle(i - 1)

        for e in range(n - 1):
            right, left = n - 1 - e, e
            self.hop(i - 1 - c, right > c, right, self.to_right, self.from_left, c == 0)
            self.hop(i - n + c, left < c, left, self.to_left, self.from_right, c == n - 1)

    def finish(self, t):
        n, c = self.n, self.c

        @pl.when(c > 0)
        def _():
            self.to_right(t, c).wait_recv()

        @pl.when(c < n - 1)
        def _():
            self.to_left(t, c).wait_recv()

        return (
            self.buf_b[t, c].astype(jnp.float32)
            + self.from_left[t, c].astype(jnp.float32)
            + self.from_right[t, c].astype(jnp.float32)
        )

    def drain(self, t):
        for d in range(self.n):

            @pl.when(d > self.c)
            def _():
                self.to_right(t, d).wait_send()

            @pl.when(d < self.c)
            def _():
                self.to_left(t, d).wait_send()


def columns(t, width):
    return pl.ds(pl.multiple_of(t * width, width), width)


def proj_kernel(
    n,
    n_smp,
    q_ref,
    kv_ref,
    suf_ref,
    suf_lse_ref,
    w_ref,
    res_ref,
    state_ref,
    out_mine,
    lse_mine,
    out_in,
    lse_in,
    attn,
    w_buf,
    buf_a,
    recv_a,
    buf_b,
    from_left,
    from_right,
    w_sem,
    os,
    orr,
    ls,
    lr,
    xs,
    xr,
    sa,
    ra,
    ss,
    rl,
    rr,
    gsr,
    gsl,
    gr,
    fs,
    fr,
):
    c, s, h = lax.axis_index("ctx"), lax.axis_index("smp"), lax.axis_index("head")
    tiles = w_buf.shape[0]
    keys, samples, per_key = suf_lse_ref.shape
    per_dest = out_mine.shape[2] // HD
    dests = per_key // per_dest
    together = 4

    greet(n, n_smp, c, s, h)

    def piece_copies(at, d):
        return (
            remote(out_mine.at[d], out_in.at[at], os.at[d], orr.at[at], {"ctx": d}),
            remote(lse_mine.at[d], lse_in.at[at], ls.at[d], lr.at[at], {"ctx": d}),
        )

    def w_copy(t):
        return pltpu.make_async_copy(w_ref.at[:, columns(t, TILE)], w_buf.at[t], w_sem.at[t])

    @pl.loop(0, tiles)
    def _(t):
        w_copy(t).start()

    lanes_at = lax.broadcasted_iota(jnp.int32, (samples, 128), 1)

    @pl.loop(0, keys)
    def _(i):
        j = lax.rem(lax.div(c, dests) + 1 + i, keys)
        key = kv_ref[0, :, columns(j, HD)]
        value = kv_ref[1, :, columns(j, HD)]
        own = q_ref[:, columns(j, per_key * HD)]
        placed = suf_ref[:, columns(j, per_key * HD)]
        placed_lse = suf_lse_ref[j]
        tables = [jnp.zeros((samples, 128), jnp.float32) for _ in range(dests)]
        for g0 in range(0, per_key, together):
            rows = jnp.concatenate(
                [own[:, g * HD : (g + 1) * HD] for g in range(g0, g0 + together)], axis=0
            )
            scores = lax.dot_general(
                rows, key, (((1,), (1,)), ((), ())), preferred_element_type=jnp.float32
            ) * HD ** (-0.5)
            high = jnp.max(scores, axis=1, keepdims=True)
            weights = jnp.exp(scores - high)
            total = jnp.sum(weights, axis=1, keepdims=True)
            summed = (
                jnp.dot(weights.astype(jnp.bfloat16), value, preferred_element_type=jnp.float32)
                / total
            )
            lse = high + jnp.log(total)
            for g in range(g0, g0 + together):
                part = slice((g - g0) * samples, (g - g0 + 1) * samples)
                own_lse, other_lse = lse[part], placed_lse[:, g : g + 1]
                top = jnp.maximum(own_lse, other_lse)
                own_weight = jnp.exp(own_lse - top)
                other_weight = jnp.exp(other_lse - top)
                both = own_weight + other_weight
                merged = (
                    own_weight * summed[part]
                    + other_weight * placed[:, g * HD : (g + 1) * HD].astype(jnp.float32)
                ) / both
                at = g % per_dest
                out_mine[j * dests + g // per_dest, :, at * HD : (at + 1) * HD] = merged.astype(
                    jnp.bfloat16
                )
                q = g // per_dest
                tables[q] = jnp.where(lanes_at == at, top + jnp.log(both), tables[q])
        for q in range(dests):
            d = j * dests + q
            lse_mine[d] = tables[q].T[:8]

            @pl.when(d != c)
            def _():
                for copy in piece_copies(c, d):
                    copy.start()

    for k in range(1, n):
        d = lax.rem(c + k, n)
        for copy in piece_copies(d, d):
            copy.wait_recv()
    for k in range(1, n):
        d = lax.rem(c + k, n)
        for copy in piece_copies(c, d):
            copy.wait_send()

    lses = [lse_mine[c]] + [lse_in[lax.rem(c + k, n)] for k in range(1, n)]
    peak = functools.reduce(jnp.maximum, lses)
    scales = [jnp.exp(value - peak) for value in lses]
    denom = functools.reduce(jnp.add, scales)
    blank = jnp.zeros((120, samples), jnp.float32)
    scales = [jnp.concatenate([value / denom, blank], axis=0).T for value in scales]
    for j in range(per_dest):
        lanes = slice(j * HD, (j + 1) * HD)
        total = scales[0][:, j : j + 1] * out_mine[c, :, lanes].astype(jnp.float32)
        for k in range(1, n):
            piece = out_in[lax.rem(c + k, n), :, lanes].astype(jnp.float32)
            total = total + scales[k][:, j : j + 1] * piece
        attn[s, :, lanes] = total.astype(jnp.bfloat16)

    def attn_copy(k):
        return remote(
            attn.at[s], attn.at[s], xs.at[k - 1], xr.at[k - 1], {"smp": lax.rem(s + k, n_smp)}
        )

    for k in range(1, n_smp):
        attn_copy(k).start()
    for k in range(1, n_smp):
        attn_copy(k).wait()

    line = Line(n, c, h, buf_a, recv_a, buf_b, from_left, from_right, sa, ra, ss, rl, rr)

    def gather_copy(t, q, way, sems):
        block = state_ref.at[q, h, :, columns(t, TILE)]
        return remote(
            block, block, sems.at[t, q], gr.at[t, q], {"ctx": lax.rem(c + way, n)}
        )

    def pass_copy(t, q):
        block = state_ref.at[q, h, :, columns(t, TILE)]
        return remote(block, block, fs.at[t, q], fr.at[t, q], {"head": 1 - h})

    def spread(t, q, right, left):
        @pl.when(right & (c < n - 1))
        def _():
            gather_copy(t, q, 1, gsr).start()

        @pl.when(left & (c > 0))
        def _():
            gather_copy(t, q, n - 1, gsl).start()

        pass_copy(t, q).start()

    @pl.loop(0, tiles + 2 * n - 1)
    def _(i):
        @pl.when(i < tiles)
        def _():
            w_copy(i).wait()
            rows = attn[...].reshape(-1, attn.shape[2])
            line.give(i, jnp.dot(rows, w_buf[i], preferred_element_type=jnp.float32))

        line.step(i)

        @pl.when((i >= n) & (i < tiles + n))
        def _():
            t = i - n
            own = line.finish(t) + res_ref[:, columns(t, TILE)].astype(jnp.float32)
            state_ref[c, h, :, columns(t, TILE)] = own.astype(jnp.bfloat16)
            spread(t, c, c >= 0, c >= 0)

        for q in range(n):
            t = i - n - lax.max(c - q, q - c)

            @pl.when((q != c) & (t >= 0) & (t < tiles))
            def _():
                gather_copy(t, q, 1, gsr).wait_recv()
                spread(t, q, q < c, q > c)

    @pl.loop(0, tiles)
    def _(t):
        line.drain(t)
        for q in range(n):

            @pl.when((q <= c) & (c < n - 1))
            def _():
                gather_copy(t, q, 1, gsr).wait_send()

            @pl.when((q >= c) & (c > 0))
            def _():
                gather_copy(t, q, n - 1, gsl).wait_send()

            pass_copy(t, q).wait()


def project(n, n_smp, queries, prefix_cache, suffix_out, suffix_lse, w, residual):
    keys, samples, per_key = suffix_lse.shape
    features = queries.shape[1] // n
    rows, width = residual.shape
    tiles = width // TILE
    vmem = pl.BlockSpec(memory_space=pltpu.VMEM)
    dma = pltpu.SemaphoreType.DMA
    bf16 = jnp.bfloat16
    return pl.pallas_call(
        functools.partial(proj_kernel, n, n_smp),
        out_shape=jax.ShapeDtypeStruct((n, 2, rows, width), bf16),
        in_specs=[vmem, vmem, vmem, vmem, pl.BlockSpec(memory_space=pl.ANY), vmem],
        out_specs=vmem,
        scratch_shapes=[
            pltpu.VMEM((n, samples, features), bf16),
            pltpu.VMEM((n, 8, samples), jnp.float32),
            pltpu.VMEM((n, samples, features), bf16),
            pltpu.VMEM((n, 8, samples), jnp.float32),
            pltpu.VMEM((n_smp, samples, features), bf16),
            pltpu.VMEM((tiles, w.shape[0], TILE), bf16),
            pltpu.VMEM((tiles, 2, n, rows, TILE), bf16),
            pltpu.VMEM((tiles, n, rows, TILE), bf16),
            pltpu.VMEM((tiles, n, rows, TILE), bf16),
            pltpu.VMEM((tiles, n, rows, TILE), bf16),
            pltpu.VMEM((tiles, n, rows, TILE), bf16),
            dma((tiles,)),
            dma((n,)),
            dma((n,)),
            dma((n,)),
            dma((n,)),
            dma((n_smp - 1,)),
            dma((n_smp - 1,)),
            dma((tiles,)),
            dma((tiles,)),
            dma((tiles, n)),
            dma((tiles, n)),
            dma((tiles, n)),
            dma((tiles, n)),
            dma((tiles, n)),
            dma((tiles, n)),
            dma((tiles, n)),
            dma((tiles, n)),
        ],
        compiler_params=pltpu.CompilerParams(
            collective_id=0, has_side_effects=True, vmem_limit_bytes=VMEM_BYTES
        ),
    )(queries, prefix_cache, suffix_out, suffix_lse, w, residual)


UNITS = 256
SLOTS = 4


def ffn_kernel(
    n,
    n_smp,
    state_ref,
    gain_ref,
    gate_ref,
    up_ref,
    down_ref,
    mixed_ref,
    scaled,
    squares,
    squares_in,
    gate_buf,
    up_buf,
    down_buf,
    part,
    part_in,
    hidden,
    buf_a,
    recv_a,
    buf_b,
    from_left,
    from_right,
    g_sem,
    u_sem,
    d_sem,
    qs,
    qr,
    ps,
    pr,
    hs,
    hr,
    sa,
    ra,
    ss,
    rl,
    rr,
):
    c, s, h = lax.axis_index("ctx"), lax.axis_index("smp"), lax.axis_index("head")
    steps = part.shape[0]
    slots = gate_buf.shape[0]
    tiles = down_buf.shape[0]
    width = state_ref.shape[3]
    all_rows = state_ref.shape[0] * 2 * state_ref.shape[2]
    smp_rows = all_rows // n_smp

    def weight_copies(t):
        slot = lax.rem(t, slots)
        return (
            pltpu.make_async_copy(
                gate_ref.at[:, columns(t, UNITS)], gate_buf.at[slot], g_sem.at[slot]
            ),
            pltpu.make_async_copy(up_ref.at[:, columns(t, UNITS)], up_buf.at[slot], u_sem.at[slot]),
        )

    def down_copy(t):
        return pltpu.make_async_copy(down_ref.at[:, columns(t, TILE)], down_buf.at[t], d_sem.at[t])

    @pl.loop(0, min(slots, steps))
    def _(t):
        for copy in weight_copies(t):
            copy.start()

    greet(n, n_smp, c, s, h)

    for block in range(n):
        wide = state_ref[block].reshape(-1, width).astype(jnp.float32)
        rows = slice(block * wide.shape[0], (block + 1) * wide.shape[0])
        scaled[rows] = (wide * gain_ref[...]).astype(jnp.bfloat16)
        sums = jnp.sum(wide * wide, axis=1, keepdims=True)
        squares[rows] = jnp.broadcast_to(sums, (wide.shape[0], 128))

    def smp_rows_of(p):
        return pl.ds(pl.multiple_of(p * smp_rows, smp_rows), smp_rows)

    def square_copy(k):
        p = lax.rem(s + k, n_smp)
        return remote(
            squares.at[smp_rows_of(p)], squares_in.at[k - 1], qs.at[k - 1], qr.at[k - 1], {"smp": p}
        )

    for k in range(1, n_smp):
        square_copy(k).start()

    def part_copy(t, k):
        p = lax.rem(s + k, n_smp)
        return remote(
            part.at[t, smp_rows_of(p)],
            part_in.at[t, k - 1],
            ps.at[t, k - 1],
            pr.at[t, k - 1],
            {"smp": p},
        )

    def hidden_copy(t, k):
        block = hidden.at[smp_rows_of(s), columns(t, UNITS)]
        return remote(
            block, block, hs.at[t, k - 1], hr.at[t, k - 1], {"smp": lax.rem(s + k, n_smp)}
        )

    def act(t):
        both = part[t, smp_rows_of(s)].astype(jnp.float32)
        for k in range(1, n_smp):
            part_copy(t, k).wait()
            both = both + part_in[t, k - 1].astype(jnp.float32)
        total = squares[smp_rows_of(s)]
        for k in range(1, n_smp):
            total = total + squares_in[k - 1]
        factor = lax.rsqrt(total / (width * n_smp) + EPSILON)[:, :1]
        gate = factor * both[:, :UNITS]
        up = factor * both[:, UNITS:]
        value = gate / (1.0 + jnp.exp(-gate)) * up
        hidden[smp_rows_of(s), columns(t, UNITS)] = value.astype(jnp.bfloat16)
        for k in range(1, n_smp):
            hidden_copy(t, k).start()

    lag = min(2, steps)

    @pl.loop(0, steps)
    def _(t):
        for copy in weight_copies(t):
            copy.wait()
        slot = lax.rem(t, slots)
        part[t, :, :UNITS] = jnp.dot(
            scaled[...], gate_buf[slot], preferred_element_type=jnp.float32
        ).astype(jnp.bfloat16)
        part[t, :, UNITS:] = jnp.dot(
            scaled[...], up_buf[slot], preferred_element_type=jnp.float32
        ).astype(jnp.bfloat16)
        for k in range(1, n_smp):
            part_copy(t, k).start()

        @pl.when(t + slots < steps)
        def _():
            for copy in weight_copies(t + slots):
                copy.start()

        @pl.when(t < tiles)
        def _():
            down_copy(t).start()

        @pl.when(t == lag)
        def _():
            for k in range(1, n_smp):
                square_copy(k).wait()

        @pl.when(t >= lag)
        def _():
            act(t - lag)

    if steps <= lag:
        for k in range(1, n_smp):
            square_copy(k).wait()

    for t in range(steps, tiles):
        down_copy(t).start()

    @pl.loop(steps - lag, steps)
    def _(t):
        act(t)

    @pl.loop(0, steps)
    def _(t):
        for k in range(1, n_smp):
            hidden_copy(t, k).wait()

    line = Line(n, c, h, buf_a, recv_a, buf_b, from_left, from_right, sa, ra, ss, rl, rr)

    @pl.loop(0, tiles + n)
    def _(i):
        @pl.when(i < tiles)
        def _():
            down_copy(i).wait()
            line.give(i, jnp.dot(hidden[...], down_buf[i], preferred_element_type=jnp.float32))

        line.step(i)

        @pl.when(i >= n)
        def _():
            t = i - n
            own = line.finish(t) + state_ref[c, h, :, columns(t, TILE)].astype(jnp.float32)
            mixed_ref[:, columns(t, TILE)] = own.astype(jnp.bfloat16)

    @pl.loop(0, tiles)
    def _(t):
        line.drain(t)


def feed_forward(n, n_smp, state, gain, gate, up, down):
    _, _, rows, width = state.shape
    all_rows = n * 2 * rows
    smp_rows = all_rows // n_smp
    units = gate.shape[1]
    steps, tiles = units // UNITS, width // TILE
    slots = min(SLOTS, steps)
    vmem = pl.BlockSpec(memory_space=pltpu.VMEM)
    hbm = pl.BlockSpec(memory_space=pl.ANY)
    dma = pltpu.SemaphoreType.DMA
    bf16 = jnp.bfloat16
    return pl.pallas_call(
        functools.partial(ffn_kernel, n, n_smp),
        out_shape=jax.ShapeDtypeStruct((rows, width), bf16),
        in_specs=[vmem, vmem, hbm, hbm, hbm],
        out_specs=vmem,
        scratch_shapes=[
            pltpu.VMEM((all_rows, width), bf16),
            pltpu.VMEM((all_rows, 128), jnp.float32),
            pltpu.VMEM((n_smp - 1, smp_rows, 128), jnp.float32),
            pltpu.VMEM((slots, width, UNITS), bf16),
            pltpu.VMEM((slots, width, UNITS), bf16),
            pltpu.VMEM((tiles, units, TILE), bf16),
            pltpu.VMEM((steps, all_rows, 2 * UNITS), bf16),
            pltpu.VMEM((steps, n_smp - 1, smp_rows, 2 * UNITS), bf16),
            pltpu.VMEM((all_rows, units), bf16),
            pltpu.VMEM((tiles, 2, n, rows, TILE), bf16),
            pltpu.VMEM((tiles, n, rows, TILE), bf16),
            pltpu.VMEM((tiles, n, rows, TILE), bf16),
            pltpu.VMEM((tiles, n, rows, TILE), bf16),
            pltpu.VMEM((tiles, n, rows, TILE), bf16),
            dma((slots,)),
            dma((slots,)),
            dma((tiles,)),
            dma((n_smp - 1,)),
            dma((n_smp - 1,)),
            dma((steps, n_smp - 1)),
            dma((steps, n_smp - 1)),
            dma((steps, n_smp - 1)),
            dma((steps, n_smp - 1)),
            dma((tiles,)),
            dma((tiles,)),
            dma((tiles, n)),
            dma((tiles, n)),
            dma((tiles, n)),
        ],
        compiler_params=pltpu.CompilerParams(
            collective_id=1, has_side_effects=True, vmem_limit_bytes=VMEM_BYTES
        ),
    )(state, gain, gate, up, down)


def on_device(
    queries,
    prefix_cache,
    suffix_cache,
    suffix_length,
    cache_sample,
    residual,
    w_out,
    norm_gain,
    gate_matrix,
    w_up,
    w_down,
):
    group_rows = queries.shape[0]
    keys_here = prefix_cache.shape[3] // HD
    heads_local = queries.shape[2] // HD
    n, n_smp = lax.axis_size("ctx"), lax.axis_size("smp")
    own_queries = queries[:, 0]
    rows_here = suffix_cache.shape[1]
    flat_index = lax.axis_index("ctx") * n_smp + lax.axis_index("smp")
    row_ids = lax.dynamic_slice_in_dim(cache_sample, flat_index * rows_here, rows_here, 0)
    local_ids = row_ids % group_rows
    row_queries = jnp.take(own_queries, local_ids, axis=0).reshape(rows_here, heads_local, HD)
    row_lengths = jnp.take(suffix_length, local_ids, axis=0)
    suffix_out, suffix_lse = suffix_piece(row_queries, suffix_cache[:, :, :, 0], row_lengths)
    chosen = local_ids[None, :] == jnp.arange(group_rows, dtype=jnp.int32)[:, None]
    placed_out = jnp.dot(
        chosen.astype(jnp.bfloat16),
        suffix_out.reshape(rows_here, -1),
        preferred_element_type=jnp.float32,
    ).astype(jnp.bfloat16)
    placed_lse = jnp.dot(
        chosen.astype(jnp.float32), suffix_lse[:, :, 0], precision=lax.Precision.HIGHEST
    )
    placed_lse = jnp.where(jnp.any(chosen, axis=1)[:, None], placed_lse, -1e30)
    placed_lse = placed_lse.reshape(group_rows, keys_here, -1).transpose(1, 0, 2)
    state = project(
        n,
        n_smp,
        own_queries,
        prefix_cache[:, :, 0],
        placed_out,
        placed_lse,
        w_out[0],
        residual,
    )
    return feed_forward(n, n_smp, state, norm_gain[None, :], gate_matrix, w_up, w_down)


def solution(mesh):
    in_specs = (
        P(("group", "smp"), "head", None),
        P(None, ("group", "ctx"), "head", None),
        P(None, ("group", "ctx", "smp"), None, "head", None),
        P(("group", "smp")),
        P("group"),
        P(("group", "ctx", "head"), "smp"),
        P("head", "ctx", "smp"),
        P("smp"),
        P("smp", ("ctx", "head")),
        P("smp", ("ctx", "head")),
        P(("ctx", "head"), "smp"),
    )
    out_specs = P(("group", "ctx", "head"), "smp")
    return jax.shard_map(
        on_device, mesh=mesh, in_specs=in_specs, out_specs=out_specs, check_vma=False
    )
```

```python
import functools

import jax
import jax.numpy as jnp
from jax import lax
from jax.experimental import pallas as pl
from jax.experimental.pallas import tpu as pltpu
from jax.sharding import PartitionSpec as P

D = 8192
QUERY_HEADS = 64
KEY_VALUE_HEADS = 8
HD = 128


EPSILON = 1e-05


def suffix_kernel(lengths_ref, queries_ref, cache_ref, out_ref, lse_ref):
    block, heads, _ = queries_ref.shape
    positions_here, width = cache_ref.shape[2:]
    per_key = heads // (width // HD)
    first = pl.program_id(0) * block
    same = (
        lax.broadcasted_iota(jnp.int32, (heads, width), 0) // per_key
        == lax.broadcasted_iota(jnp.int32, (heads, width), 1) // HD
    )
    positions = lax.broadcasted_iota(jnp.int32, (heads, positions_here), 1)
    for r in range(block):
        q = queries_ref[r].astype(jnp.float32)
        spread = jnp.concatenate([q] * (width // HD), axis=1)
        spread = jnp.where(same, spread, 0.0).astype(jnp.bfloat16)
        scores = lax.dot_general(
            spread, cache_ref[0, r], (((1,), (1,)), ((), ())), preferred_element_type=jnp.float32
        )
        scores = jnp.where(positions < lengths_ref[first + r], scores * HD ** (-0.5), -jnp.inf)
        high = jnp.max(scores, axis=1, keepdims=True)
        weights = jnp.exp(scores - high)
        total = jnp.sum(weights, axis=1, keepdims=True)
        summed = jnp.dot(
            weights.astype(jnp.bfloat16), cache_ref[1, r], preferred_element_type=jnp.float32
        )
        own = jnp.concatenate(
            [
                summed[j * per_key : (j + 1) * per_key, j * HD : (j + 1) * HD]
                for j in range(width // HD)
            ],
            axis=0,
        )
        out_ref[r] = (own / total).astype(jnp.bfloat16)
        lse_ref[r] = high + jnp.log(total)


def suffix_piece(row_queries, suffix_cache, row_lengths):
    rows, heads, _ = row_queries.shape
    block = min(8, rows)
    _, _, positions_here, width = suffix_cache.shape
    return pl.pallas_call(
        suffix_kernel,
        grid=(rows // block,),
        out_shape=(
            jax.ShapeDtypeStruct((rows, heads, HD), jnp.bfloat16),
            jax.ShapeDtypeStruct((rows, heads, 1), jnp.float32),
        ),
        in_specs=[
            pl.BlockSpec(memory_space=pltpu.SMEM),
            pl.BlockSpec((block, heads, HD), lambda i: (i, 0, 0)),
            pl.BlockSpec((2, block, positions_here, width), lambda i: (0, i, 0, 0)),
        ],
        out_specs=(
            pl.BlockSpec((block, heads, HD), lambda i: (i, 0, 0)),
            pl.BlockSpec((block, heads, 1), lambda i: (i, 0, 0)),
        ),
        compiler_params=pltpu.CompilerParams(vmem_limit_bytes=VMEM_BYTES),
    )(row_lengths, row_queries, suffix_cache)


MESH = pl.DeviceIdType.MESH
TILE = 512
LAG = 3
VMEM_BYTES = 62 * 1024 * 1024


def remote(src, dst, send_sem, recv_sem, where):
    return pltpu.make_async_remote_copy(
        src_ref=src,
        dst_ref=dst,
        send_sem=send_sem,
        recv_sem=recv_sem,
        device_id=where,
        device_id_type=MESH,
    )


def greet(n, n_smp, c, s, h):
    barrier = pltpu.get_barrier_semaphore()
    for k in range(1, n):
        pl.semaphore_signal(barrier, inc=1, device_id={"ctx": lax.rem(c + k, n)}, device_id_type=MESH)
    for k in range(1, n_smp):
        pl.semaphore_signal(
            barrier, inc=1, device_id={"smp": lax.rem(s + k, n_smp)}, device_id_type=MESH
        )
    pl.semaphore_signal(barrier, inc=1, device_id={"head": 1 - h}, device_id_type=MESH)
    pl.semaphore_wait(barrier, (n - 1) + (n_smp - 1) + 1)


class Scatter:
    def __init__(self, n, c, h, buf_a, recv_a, buf_b, recv_b, sa, ra, sb, rb):
        self.n, self.c, self.h = n, c, h
        self.buf_a, self.recv_a, self.buf_b, self.recv_b = buf_a, recv_a, buf_b, recv_b
        self.sa, self.ra, self.sb, self.rb = sa, ra, sb, rb

    def pair_copy(self, t):
        return remote(
            self.buf_a.at[t, 1 - self.h],
            self.recv_a.at[t],
            self.sa.at[t],
            self.ra.at[t],
            {"head": 1 - self.h},
        )

    def row_copy(self, t, k):
        d = lax.rem(self.c + k, self.n)
        return remote(
            self.buf_b.at[t, d],
            self.recv_b.at[t, k - 1],
            self.sb.at[t, k - 1],
            self.rb.at[t, k - 1],
            {"ctx": d},
        )

    def give(self, t, value):
        _, _, n, rows, width = self.buf_a.shape
        parts = value.reshape(n, 2, rows, width).astype(jnp.bfloat16)
        self.buf_a[t, 0] = parts[:, 0]
        self.buf_a[t, 1] = parts[:, 1]
        self.pair_copy(t).start()

    def middle(self, t):
        self.pair_copy(t).wait()
        both = self.buf_a[t, self.h].astype(jnp.float32) + self.recv_a[t].astype(jnp.float32)
        self.buf_b[t] = both.astype(jnp.bfloat16)
        for k in range(1, self.n):
            self.row_copy(t, k).start()

    def finish(self, t):
        total = self.buf_b[t, self.c].astype(jnp.float32)
        for k in range(1, self.n):
            self.row_copy(t, k).wait()
            total = total + self.recv_b[t, k - 1].astype(jnp.float32)
        return total


def columns(t, width):
    return pl.ds(pl.multiple_of(t * width, width), width)


def proj_kernel(
    n,
    n_smp,
    q_ref,
    kv_ref,
    suf_ref,
    suf_lse_ref,
    w_ref,
    res_ref,
    state_ref,
    out_mine,
    lse_mine,
    out_in,
    lse_in,
    attn,
    w_buf,
    buf_a,
    recv_a,
    buf_b,
    recv_b,
    w_sem,
    os,
    orr,
    ls,
    lr,
    xs,
    xr,
    sa,
    ra,
    sb,
    rb,
    gsr,
    gsl,
    gr,
    fs,
    fr,
):
    c, s, h = lax.axis_index("ctx"), lax.axis_index("smp"), lax.axis_index("head")
    tiles = w_buf.shape[0]
    keys, samples, per_key = suf_lse_ref.shape
    per_dest = out_mine.shape[2] // HD
    dests = per_key // per_dest
    together = 4

    greet(n, n_smp, c, s, h)

    def piece_copies(at, d):
        return (
            remote(out_mine.at[d], out_in.at[at], os.at[d], orr.at[at], {"ctx": d}),
            remote(lse_mine.at[d], lse_in.at[at], ls.at[d], lr.at[at], {"ctx": d}),
        )

    def w_copy(t):
        return pltpu.make_async_copy(w_ref.at[:, columns(t, TILE)], w_buf.at[t], w_sem.at[t])

    @pl.loop(0, tiles)
    def _(t):
        w_copy(t).start()

    lanes_at = lax.broadcasted_iota(jnp.int32, (samples, 128), 1)

    @pl.loop(0, keys)
    def _(i):
        j = lax.rem(lax.div(c, dests) + 1 + i, keys)
        key = kv_ref[0, :, columns(j, HD)]
        value = kv_ref[1, :, columns(j, HD)]
        own = q_ref[:, columns(j, per_key * HD)]
        placed = suf_ref[:, columns(j, per_key * HD)]
        placed_lse = suf_lse_ref[j]
        tables = [jnp.zeros((samples, 128), jnp.float32) for _ in range(dests)]
        for g0 in range(0, per_key, together):
            rows = jnp.concatenate(
                [own[:, g * HD : (g + 1) * HD] for g in range(g0, g0 + together)], axis=0
            )
            scores = lax.dot_general(
                rows, key, (((1,), (1,)), ((), ())), preferred_element_type=jnp.float32
            ) * HD ** (-0.5)
            high = jnp.max(scores, axis=1, keepdims=True)
            weights = jnp.exp(scores - high)
            total = jnp.sum(weights, axis=1, keepdims=True)
            summed = (
                jnp.dot(weights.astype(jnp.bfloat16), value, preferred_element_type=jnp.float32)
                / total
            )
            lse = high + jnp.log(total)
            for g in range(g0, g0 + together):
                part = slice((g - g0) * samples, (g - g0 + 1) * samples)
                own_lse, other_lse = lse[part], placed_lse[:, g : g + 1]
                top = jnp.maximum(own_lse, other_lse)
                own_weight = jnp.exp(own_lse - top)
                other_weight = jnp.exp(other_lse - top)
                both = own_weight + other_weight
                merged = (
                    own_weight * summed[part]
                    + other_weight * placed[:, g * HD : (g + 1) * HD].astype(jnp.float32)
                ) / both
                at = g % per_dest
                out_mine[j * dests + g // per_dest, :, at * HD : (at + 1) * HD] = merged.astype(
                    jnp.bfloat16
                )
                q = g // per_dest
                tables[q] = jnp.where(lanes_at == at, top + jnp.log(both), tables[q])
        for q in range(dests):
            d = j * dests + q
            lse_mine[d] = tables[q].T[:8]

            @pl.when(d != c)
            def _():
                for copy in piece_copies(c, d):
                    copy.start()

    for k in range(1, n):
        d = lax.rem(c + k, n)
        for copy in piece_copies(d, d):
            copy.wait_recv()
    for k in range(1, n):
        d = lax.rem(c + k, n)
        for copy in piece_copies(c, d):
            copy.wait_send()

    lses = [lse_mine[c]] + [lse_in[lax.rem(c + k, n)] for k in range(1, n)]
    peak = functools.reduce(jnp.maximum, lses)
    scales = [jnp.exp(value - peak) for value in lses]
    denom = functools.reduce(jnp.add, scales)
    blank = jnp.zeros((120, samples), jnp.float32)
    scales = [jnp.concatenate([value / denom, blank], axis=0).T for value in scales]
    for j in range(per_dest):
        lanes = slice(j * HD, (j + 1) * HD)
        total = scales[0][:, j : j + 1] * out_mine[c, :, lanes].astype(jnp.float32)
        for k in range(1, n):
            piece = out_in[lax.rem(c + k, n), :, lanes].astype(jnp.float32)
            total = total + scales[k][:, j : j + 1] * piece
        attn[s, :, lanes] = total.astype(jnp.bfloat16)

    def attn_copy(k):
        return remote(
            attn.at[s], attn.at[s], xs.at[k - 1], xr.at[k - 1], {"smp": lax.rem(s + k, n_smp)}
        )

    for k in range(1, n_smp):
        attn_copy(k).start()
    for k in range(1, n_smp):
        attn_copy(k).wait()

    scatter = Scatter(n, c, h, buf_a, recv_a, buf_b, recv_b, sa, ra, sb, rb)

    def gather_copy(t, q, way, sems):
        block = state_ref.at[q, h, :, columns(t, TILE)]
        return remote(
            block, block, sems.at[t, q], gr.at[t, q], {"ctx": lax.rem(c + way, n)}
        )

    def pass_copy(t, q):
        block = state_ref.at[q, h, :, columns(t, TILE)]
        return remote(block, block, fs.at[t, q], fr.at[t, q], {"head": 1 - h})

    def spread(t, q, right, left):
        @pl.when(right & (c < n - 1))
        def _():
            gather_copy(t, q, 1, gsr).start()

        @pl.when(left & (c > 0))
        def _():
            gather_copy(t, q, n - 1, gsl).start()

        pass_copy(t, q).start()

    @pl.loop(0, tiles + LAG + n - 1)
    def _(i):
        @pl.when(i < tiles)
        def _():
            w_copy(i).wait()
            rows = attn[...].reshape(-1, attn.shape[2])
            scatter.give(i, jnp.dot(rows, w_buf[i], preferred_element_type=jnp.float32))

        @pl.when((i >= 1) & (i <= tiles))
        def _():
            scatter.middle(i - 1)

        @pl.when((i >= LAG) & (i < tiles + LAG))
        def _():
            t = i - LAG
            own = scatter.finish(t) + res_ref[:, columns(t, TILE)].astype(jnp.float32)
            state_ref[c, h, :, columns(t, TILE)] = own.astype(jnp.bfloat16)
            spread(t, c, c >= 0, c >= 0)

        for q in range(n):
            t = i - LAG - lax.max(c - q, q - c)

            @pl.when((q != c) & (t >= 0) & (t < tiles))
            def _():
                gather_copy(t, q, 1, gsr).wait_recv()
                spread(t, q, q < c, q > c)

    @pl.loop(0, tiles)
    def _(t):
        for q in range(n):

            @pl.when((q <= c) & (c < n - 1))
            def _():
                gather_copy(t, q, 1, gsr).wait_send()

            @pl.when((q >= c) & (c > 0))
            def _():
                gather_copy(t, q, n - 1, gsl).wait_send()

            pass_copy(t, q).wait()


def project(n, n_smp, queries, prefix_cache, suffix_out, suffix_lse, w, residual):
    keys, samples, per_key = suffix_lse.shape
    features = queries.shape[1] // n
    rows, width = residual.shape
    tiles = width // TILE
    vmem = pl.BlockSpec(memory_space=pltpu.VMEM)
    dma = pltpu.SemaphoreType.DMA
    bf16 = jnp.bfloat16
    return pl.pallas_call(
        functools.partial(proj_kernel, n, n_smp),
        out_shape=jax.ShapeDtypeStruct((n, 2, rows, width), bf16),
        in_specs=[vmem, vmem, vmem, vmem, pl.BlockSpec(memory_space=pl.ANY), vmem],
        out_specs=vmem,
        scratch_shapes=[
            pltpu.VMEM((n, samples, features), bf16),
            pltpu.VMEM((n, 8, samples), jnp.float32),
            pltpu.VMEM((n, samples, features), bf16),
            pltpu.VMEM((n, 8, samples), jnp.float32),
            pltpu.VMEM((n_smp, samples, features), bf16),
            pltpu.VMEM((tiles, w.shape[0], TILE), bf16),
            pltpu.VMEM((tiles, 2, n, rows, TILE), bf16),
            pltpu.VMEM((tiles, n, rows, TILE), bf16),
            pltpu.VMEM((tiles, n, rows, TILE), bf16),
            pltpu.VMEM((tiles, n - 1, rows, TILE), bf16),
            dma((tiles,)),
            dma((n,)),
            dma((n,)),
            dma((n,)),
            dma((n,)),
            dma((n_smp - 1,)),
            dma((n_smp - 1,)),
            dma((tiles,)),
            dma((tiles,)),
            dma((tiles, n - 1)),
            dma((tiles, n - 1)),
            dma((tiles, n)),
            dma((tiles, n)),
            dma((tiles, n)),
            dma((tiles, n)),
            dma((tiles, n)),
        ],
        compiler_params=pltpu.CompilerParams(
            collective_id=0, has_side_effects=True, vmem_limit_bytes=VMEM_BYTES
        ),
    )(queries, prefix_cache, suffix_out, suffix_lse, w, residual)


UNITS = 256
SLOTS = 4


def ffn_kernel(
    n,
    n_smp,
    state_ref,
    gain_ref,
    gate_ref,
    up_ref,
    down_ref,
    mixed_ref,
    scaled,
    squares,
    squares_in,
    gate_buf,
    up_buf,
    down_buf,
    part,
    part_in,
    hidden,
    buf_a,
    recv_a,
    buf_b,
    recv_b,
    g_sem,
    u_sem,
    d_sem,
    qs,
    qr,
    ps,
    pr,
    hs,
    hr,
    sa,
    ra,
    sb,
    rb,
):
    c, s, h = lax.axis_index("ctx"), lax.axis_index("smp"), lax.axis_index("head")
    steps = part.shape[0]
    slots = gate_buf.shape[0]
    tiles = down_buf.shape[0]
    width = state_ref.shape[3]
    all_rows = state_ref.shape[0] * 2 * state_ref.shape[2]
    smp_rows = all_rows // n_smp

    def weight_copies(t):
        slot = lax.rem(t, slots)
        return (
            pltpu.make_async_copy(
                gate_ref.at[:, columns(t, UNITS)], gate_buf.at[slot], g_sem.at[slot]
            ),
            pltpu.make_async_copy(up_ref.at[:, columns(t, UNITS)], up_buf.at[slot], u_sem.at[slot]),
        )

    def down_copy(t):
        return pltpu.make_async_copy(down_ref.at[:, columns(t, TILE)], down_buf.at[t], d_sem.at[t])

    @pl.loop(0, min(slots, steps))
    def _(t):
        for copy in weight_copies(t):
            copy.start()

    greet(n, n_smp, c, s, h)

    for block in range(n):
        wide = state_ref[block].reshape(-1, width).astype(jnp.float32)
        rows = slice(block * wide.shape[0], (block + 1) * wide.shape[0])
        scaled[rows] = (wide * gain_ref[...]).astype(jnp.bfloat16)
        sums = jnp.sum(wide * wide, axis=1, keepdims=True)
        squares[rows] = jnp.broadcast_to(sums, (wide.shape[0], 128))

    def smp_rows_of(p):
        return pl.ds(pl.multiple_of(p * smp_rows, smp_rows), smp_rows)

    def square_copy(k):
        p = lax.rem(s + k, n_smp)
        return remote(
            squares.at[smp_rows_of(p)], squares_in.at[k - 1], qs.at[k - 1], qr.at[k - 1], {"smp": p}
        )

    for k in range(1, n_smp):
        square_copy(k).start()

    def part_copy(t, k):
        p = lax.rem(s + k, n_smp)
        return remote(
            part.at[t, smp_rows_of(p)],
            part_in.at[t, k - 1],
            ps.at[t, k - 1],
            pr.at[t, k - 1],
            {"smp": p},
        )

    def hidden_copy(t, k):
        block = hidden.at[smp_rows_of(s), columns(t, UNITS)]
        return remote(
            block, block, hs.at[t, k - 1], hr.at[t, k - 1], {"smp": lax.rem(s + k, n_smp)}
        )

    def act(t):
        both = part[t, smp_rows_of(s)].astype(jnp.float32)
        for k in range(1, n_smp):
            part_copy(t, k).wait()
            both = both + part_in[t, k - 1].astype(jnp.float32)
        total = squares[smp_rows_of(s)]
        for k in range(1, n_smp):
            total = total + squares_in[k - 1]
        factor = lax.rsqrt(total / (width * n_smp) + EPSILON)[:, :1]
        gate = factor * both[:, :UNITS]
        up = factor * both[:, UNITS:]
        value = gate / (1.0 + jnp.exp(-gate)) * up
        hidden[smp_rows_of(s), columns(t, UNITS)] = value.astype(jnp.bfloat16)
        for k in range(1, n_smp):
            hidden_copy(t, k).start()

    lag = min(2, steps)

    @pl.loop(0, steps)
    def _(t):
        for copy in weight_copies(t):
            copy.wait()
        slot = lax.rem(t, slots)
        part[t, :, :UNITS] = jnp.dot(
            scaled[...], gate_buf[slot], preferred_element_type=jnp.float32
        ).astype(jnp.bfloat16)
        part[t, :, UNITS:] = jnp.dot(
            scaled[...], up_buf[slot], preferred_element_type=jnp.float32
        ).astype(jnp.bfloat16)
        for k in range(1, n_smp):
            part_copy(t, k).start()

        @pl.when(t + slots < steps)
        def _():
            for copy in weight_copies(t + slots):
                copy.start()

        @pl.when(t < tiles)
        def _():
            down_copy(t).start()

        @pl.when(t == lag)
        def _():
            for k in range(1, n_smp):
                square_copy(k).wait()

        @pl.when(t >= lag)
        def _():
            act(t - lag)

    if steps <= lag:
        for k in range(1, n_smp):
            square_copy(k).wait()

    for t in range(steps, tiles):
        down_copy(t).start()

    @pl.loop(steps - lag, steps)
    def _(t):
        act(t)

    @pl.loop(0, steps)
    def _(t):
        for k in range(1, n_smp):
            hidden_copy(t, k).wait()

    scatter = Scatter(n, c, h, buf_a, recv_a, buf_b, recv_b, sa, ra, sb, rb)

    @pl.loop(0, tiles)
    def _(t):
        down_copy(t).wait()
        scatter.give(t, jnp.dot(hidden[...], down_buf[t], preferred_element_type=jnp.float32))

        @pl.when(t >= 1)
        def _():
            scatter.middle(t - 1)

    scatter.middle(tiles - 1)

    @pl.loop(0, tiles)
    def _(t):
        own = scatter.finish(t) + state_ref[c, h, :, columns(t, TILE)].astype(jnp.float32)
        mixed_ref[:, columns(t, TILE)] = own.astype(jnp.bfloat16)


def feed_forward(n, n_smp, state, gain, gate, up, down):
    _, _, rows, width = state.shape
    all_rows = n * 2 * rows
    smp_rows = all_rows // n_smp
    units = gate.shape[1]
    steps, tiles = units // UNITS, width // TILE
    slots = min(SLOTS, steps)
    vmem = pl.BlockSpec(memory_space=pltpu.VMEM)
    hbm = pl.BlockSpec(memory_space=pl.ANY)
    dma = pltpu.SemaphoreType.DMA
    bf16 = jnp.bfloat16
    return pl.pallas_call(
        functools.partial(ffn_kernel, n, n_smp),
        out_shape=jax.ShapeDtypeStruct((rows, width), bf16),
        in_specs=[vmem, vmem, hbm, hbm, hbm],
        out_specs=vmem,
        scratch_shapes=[
            pltpu.VMEM((all_rows, width), bf16),
            pltpu.VMEM((all_rows, 128), jnp.float32),
            pltpu.VMEM((n_smp - 1, smp_rows, 128), jnp.float32),
            pltpu.VMEM((slots, width, UNITS), bf16),
            pltpu.VMEM((slots, width, UNITS), bf16),
            pltpu.VMEM((tiles, units, TILE), bf16),
            pltpu.VMEM((steps, all_rows, 2 * UNITS), bf16),
            pltpu.VMEM((steps, n_smp - 1, smp_rows, 2 * UNITS), bf16),
            pltpu.VMEM((all_rows, units), bf16),
            pltpu.VMEM((tiles, 2, n, rows, TILE), bf16),
            pltpu.VMEM((tiles, n, rows, TILE), bf16),
            pltpu.VMEM((tiles, n, rows, TILE), bf16),
            pltpu.VMEM((tiles, n - 1, rows, TILE), bf16),
            dma((slots,)),
            dma((slots,)),
            dma((tiles,)),
            dma((n_smp - 1,)),
            dma((n_smp - 1,)),
            dma((steps, n_smp - 1)),
            dma((steps, n_smp - 1)),
            dma((steps, n_smp - 1)),
            dma((steps, n_smp - 1)),
            dma((tiles,)),
            dma((tiles,)),
            dma((tiles, n - 1)),
            dma((tiles, n - 1)),
        ],
        compiler_params=pltpu.CompilerParams(
            collective_id=1, has_side_effects=True, vmem_limit_bytes=VMEM_BYTES
        ),
    )(state, gain, gate, up, down)


def on_device(
    queries,
    prefix_cache,
    suffix_cache,
    suffix_length,
    cache_sample,
    residual,
    w_out,
    norm_gain,
    gate_matrix,
    w_up,
    w_down,
):
    group_rows = queries.shape[0]
    keys_here = prefix_cache.shape[3] // HD
    heads_local = queries.shape[2] // HD
    n, n_smp = lax.axis_size("ctx"), lax.axis_size("smp")
    own_queries = queries[:, 0]
    rows_here = suffix_cache.shape[1]
    flat_index = lax.axis_index("ctx") * n_smp + lax.axis_index("smp")
    row_ids = lax.dynamic_slice_in_dim(cache_sample, flat_index * rows_here, rows_here, 0)
    local_ids = row_ids % group_rows
    chosen = local_ids[None, :] == jnp.arange(group_rows, dtype=jnp.int32)[:, None]
    row_queries = jnp.dot(
        chosen.T.astype(jnp.bfloat16), own_queries, preferred_element_type=jnp.float32
    ).astype(jnp.bfloat16)
    row_queries = row_queries.reshape(rows_here, heads_local, HD)
    row_lengths = jnp.sum(jnp.where(chosen, suffix_length[:, None], 0), axis=0)
    suffix_out, suffix_lse = suffix_piece(row_queries, suffix_cache[:, :, :, 0], row_lengths)
    placed_out = jnp.dot(
        chosen.astype(jnp.bfloat16),
        suffix_out.reshape(rows_here, -1),
        preferred_element_type=jnp.float32,
    ).astype(jnp.bfloat16)
    placed_lse = jnp.dot(
        chosen.astype(jnp.float32), suffix_lse[:, :, 0], precision=lax.Precision.HIGHEST
    )
    placed_lse = jnp.where(jnp.any(chosen, axis=1)[:, None], placed_lse, -1e30)
    placed_lse = placed_lse.reshape(group_rows, keys_here, -1).transpose(1, 0, 2)
    state = project(
        n,
        n_smp,
        own_queries,
        prefix_cache[:, :, 0],
        placed_out,
        placed_lse,
        w_out[0],
        residual,
    )
    return feed_forward(n, n_smp, state, norm_gain[None, :], gate_matrix, w_up, w_down)


def solution(mesh):
    in_specs = (
        P(("group", "smp"), "head", None),
        P(None, ("group", "ctx"), "head", None),
        P(None, ("group", "ctx", "smp"), None, "head", None),
        P(("group", "smp")),
        P("group"),
        P(("group", "ctx", "head"), "smp"),
        P("head", "ctx", "smp"),
        P("smp"),
        P("smp", ("ctx", "head")),
        P("smp", ("ctx", "head")),
        P(("ctx", "head"), "smp"),
    )
    out_specs = P(("group", "ctx", "head"), "smp")
    return jax.shard_map(
        on_device, mesh=mesh, in_specs=in_specs, out_specs=out_specs, check_vma=False
    )
```

```python
import functools

import jax
import jax.numpy as jnp
from jax import lax
from jax.experimental import pallas as pl
from jax.experimental.pallas import tpu as pltpu
from jax.sharding import PartitionSpec as P

D = 8192
QUERY_HEADS = 64
KEY_VALUE_HEADS = 8
HD = 128


EPSILON = 1e-05


def suffix_kernel(lengths_ref, queries_ref, cache_ref, out_ref, lse_ref):
    block, heads, _ = queries_ref.shape
    positions_here, width = cache_ref.shape[2:]
    per_key = heads // (width // HD)
    first = pl.program_id(0) * block
    same = (
        lax.broadcasted_iota(jnp.int32, (heads, width), 0) // per_key
        == lax.broadcasted_iota(jnp.int32, (heads, width), 1) // HD
    )
    positions = lax.broadcasted_iota(jnp.int32, (heads, positions_here), 1)
    for r in range(block):
        q = queries_ref[r].astype(jnp.float32)
        spread = jnp.concatenate([q] * (width // HD), axis=1)
        spread = jnp.where(same, spread, 0.0).astype(jnp.bfloat16)
        scores = lax.dot_general(
            spread, cache_ref[0, r], (((1,), (1,)), ((), ())), preferred_element_type=jnp.float32
        )
        scores = jnp.where(positions < lengths_ref[first + r], scores * HD ** (-0.5), -jnp.inf)
        high = jnp.max(scores, axis=1, keepdims=True)
        weights = jnp.exp(scores - high)
        total = jnp.sum(weights, axis=1, keepdims=True)
        summed = jnp.dot(
            weights.astype(jnp.bfloat16), cache_ref[1, r], preferred_element_type=jnp.float32
        )
        own = jnp.concatenate(
            [
                summed[j * per_key : (j + 1) * per_key, j * HD : (j + 1) * HD]
                for j in range(width // HD)
            ],
            axis=0,
        )
        out_ref[r] = (own / total).astype(jnp.bfloat16)
        lse_ref[r] = high + jnp.log(total)


def suffix_piece(row_queries, suffix_cache, row_lengths):
    rows, heads, _ = row_queries.shape
    block = min(8, rows)
    _, _, positions_here, width = suffix_cache.shape
    return pl.pallas_call(
        suffix_kernel,
        grid=(rows // block,),
        out_shape=(
            jax.ShapeDtypeStruct((rows, heads, HD), jnp.bfloat16),
            jax.ShapeDtypeStruct((rows, heads, 1), jnp.float32),
        ),
        in_specs=[
            pl.BlockSpec(memory_space=pltpu.SMEM),
            pl.BlockSpec((block, heads, HD), lambda i: (i, 0, 0)),
            pl.BlockSpec((2, block, positions_here, width), lambda i: (0, i, 0, 0)),
        ],
        out_specs=(
            pl.BlockSpec((block, heads, HD), lambda i: (i, 0, 0)),
            pl.BlockSpec((block, heads, 1), lambda i: (i, 0, 0)),
        ),
        compiler_params=pltpu.CompilerParams(vmem_limit_bytes=57 * 1024 * 1024),
    )(row_lengths, row_queries, suffix_cache)


MESH = pl.DeviceIdType.MESH
TILE = 512
VMEM_BYTES = 62 * 1024 * 1024


def remote(src, dst, send_sem, recv_sem, where):
    return pltpu.make_async_remote_copy(
        src_ref=src,
        dst_ref=dst,
        send_sem=send_sem,
        recv_sem=recv_sem,
        device_id=where,
        device_id_type=MESH,
    )


def greet(n, n_smp, c, s, h):
    barrier = pltpu.get_barrier_semaphore()
    for k in range(1, n):
        pl.semaphore_signal(barrier, inc=1, device_id={"ctx": lax.rem(c + k, n)}, device_id_type=MESH)
    for k in range(1, n_smp):
        pl.semaphore_signal(
            barrier, inc=1, device_id={"smp": lax.rem(s + k, n_smp)}, device_id_type=MESH
        )
    pl.semaphore_signal(barrier, inc=1, device_id={"head": 1 - h}, device_id_type=MESH)
    pl.semaphore_wait(barrier, (n - 1) + (n_smp - 1) + 1)


class Line:
    def __init__(self, n, c, h, buf_a, recv_a, buf_b, from_left, from_right, sa, ra, ss, rl, rr):
        self.n, self.c, self.h = n, c, h
        self.buf_a, self.recv_a, self.buf_b = buf_a, recv_a, buf_b
        self.from_left, self.from_right = from_left, from_right
        self.sa, self.ra, self.ss, self.rl, self.rr = sa, ra, ss, rl, rr
        self.tiles = buf_a.shape[0]

        @pl.when(c == 0)
        def _():
            from_left[:, 0] = jnp.zeros(from_left.shape[:1] + from_left.shape[2:], from_left.dtype)

        @pl.when(c == n - 1)
        def _():
            from_right[:, n - 1] = jnp.zeros(
                from_right.shape[:1] + from_right.shape[2:], from_right.dtype
            )

    def pair_copy(self, t):
        return remote(
            self.buf_a.at[t, 1 - self.h],
            self.recv_a.at[t],
            self.sa.at[t],
            self.ra.at[t],
            {"head": 1 - self.h},
        )

    def to_right(self, t, d):
        return remote(
            self.buf_b.at[t, d],
            self.from_left.at[t, d],
            self.ss.at[t, d],
            self.rl.at[t, d],
            {"ctx": lax.rem(self.c + 1, self.n)},
        )

    def to_left(self, t, d):
        return remote(
            self.buf_b.at[t, d],
            self.from_right.at[t, d],
            self.ss.at[t, d],
            self.rr.at[t, d],
            {"ctx": lax.rem(self.c + self.n - 1, self.n)},
        )

    def give(self, t, value):
        _, _, n, rows, width = self.buf_a.shape
        parts = value.reshape(n, 2, rows, width).astype(jnp.bfloat16)
        self.buf_a[t, 0] = parts[:, 0]
        self.buf_a[t, 1] = parts[:, 1]
        self.pair_copy(t).start()

    def middle(self, t):
        self.pair_copy(t).wait()
        both = self.buf_a[t, self.h].astype(jnp.float32) + self.recv_a[t].astype(jnp.float32)
        self.buf_b[t] = both.astype(jnp.bfloat16)

    def hop(self, t, inside, d, copy_of, arrived, first):
        @pl.when(inside & (t >= 0) & (t < self.tiles))
        def _():
            @pl.when(jnp.logical_not(first))
            def _():
                copy_of(t, d).wait_recv()
                both = self.buf_b[t, d].astype(jnp.float32) + arrived[t, d].astype(jnp.float32)
                self.buf_b[t, d] = both.astype(jnp.bfloat16)

            copy_of(t, d).start()

    def step(self, i):
        n, c = self.n, self.c

        @pl.when((i >= 1) & (i <= self.tiles))
        def _():
            self.middle(i - 1)

        for e in range(n - 1):
            right, left = n - 1 - e, e
            self.hop(i - 1 - c, right > c, right, self.to_right, self.from_left, c == 0)
            self.hop(i - n + c, left < c, left, self.to_left, self.from_right, c == n - 1)

    def finish(self, t):
        n, c = self.n, self.c

        @pl.when(c > 0)
        def _():
            self.to_right(t, c).wait_recv()

        @pl.when(c < n - 1)
        def _():
            self.to_left(t, c).wait_recv()

        return (
            self.buf_b[t, c].astype(jnp.float32)
            + self.from_left[t, c].astype(jnp.float32)
            + self.from_right[t, c].astype(jnp.float32)
        )

    def drain(self, t):
        for d in range(self.n):

            @pl.when(d > self.c)
            def _():
                self.to_right(t, d).wait_send()

            @pl.when(d < self.c)
            def _():
                self.to_left(t, d).wait_send()


class Scatter:
    def __init__(self, n, c, h, buf_a, recv_a, buf_b, recv_b, sa, ra, sb, rb):
        self.n, self.c, self.h = n, c, h
        self.buf_a, self.recv_a, self.buf_b, self.recv_b = buf_a, recv_a, buf_b, recv_b
        self.sa, self.ra, self.sb, self.rb = sa, ra, sb, rb

    def pair_copy(self, t):
        return remote(
            self.buf_a.at[t, 1 - self.h],
            self.recv_a.at[t],
            self.sa.at[t],
            self.ra.at[t],
            {"head": 1 - self.h},
        )

    def row_copy(self, t, k):
        d = lax.rem(self.c + k, self.n)
        return remote(
            self.buf_b.at[t, d],
            self.recv_b.at[t, k - 1],
            self.sb.at[t, k - 1],
            self.rb.at[t, k - 1],
            {"ctx": d},
        )

    def give(self, t, value):
        _, _, n, rows, width = self.buf_a.shape
        parts = value.reshape(n, 2, rows, width).astype(jnp.bfloat16)
        self.buf_a[t, 0] = parts[:, 0]
        self.buf_a[t, 1] = parts[:, 1]
        self.pair_copy(t).start()

    def middle(self, t):
        self.pair_copy(t).wait()
        both = self.buf_a[t, self.h].astype(jnp.float32) + self.recv_a[t].astype(jnp.float32)
        self.buf_b[t] = both.astype(jnp.bfloat16)
        for k in range(1, self.n):
            self.row_copy(t, k).start()

    def finish(self, t):
        total = self.buf_b[t, self.c].astype(jnp.float32)
        for k in range(1, self.n):
            self.row_copy(t, k).wait()
            total = total + self.recv_b[t, k - 1].astype(jnp.float32)
        return total


def columns(t, width):
    return pl.ds(pl.multiple_of(t * width, width), width)


def proj_kernel(
    n,
    n_smp,
    q_ref,
    kv_ref,
    suf_ref,
    suf_lse_ref,
    w_ref,
    res_ref,
    state_ref,
    out_mine,
    lse_mine,
    out_in,
    lse_in,
    attn,
    w_buf,
    buf_a,
    recv_a,
    buf_b,
    from_left,
    from_right,
    w_sem,
    os,
    orr,
    ls,
    lr,
    xs,
    xr,
    sa,
    ra,
    ss,
    rl,
    rr,
    gsr,
    gsl,
    gr,
    fs,
    fr,
):
    c, s, h = lax.axis_index("ctx"), lax.axis_index("smp"), lax.axis_index("head")
    tiles = w_buf.shape[0]
    keys, samples, per_key = suf_lse_ref.shape
    per_dest = out_mine.shape[2] // HD
    dests = per_key // per_dest
    together = 4

    greet(n, n_smp, c, s, h)

    def piece_copies(at, d):
        return (
            remote(out_mine.at[d], out_in.at[at], os.at[d], orr.at[at], {"ctx": d}),
            remote(lse_mine.at[d], lse_in.at[at], ls.at[d], lr.at[at], {"ctx": d}),
        )

    def w_copy(t):
        return pltpu.make_async_copy(w_ref.at[:, columns(t, TILE)], w_buf.at[t], w_sem.at[t])

    @pl.loop(0, tiles)
    def _(t):
        w_copy(t).start()

    lanes_at = lax.broadcasted_iota(jnp.int32, (samples, 128), 1)

    @pl.loop(0, keys)
    def _(i):
        j = lax.rem(lax.div(c, dests) + 1 + i, keys)
        key = kv_ref[0, :, columns(j, HD)]
        value = kv_ref[1, :, columns(j, HD)]
        own = q_ref[:, columns(j, per_key * HD)]
        placed = suf_ref[:, columns(j, per_key * HD)]
        placed_lse = suf_lse_ref[j]
        tables = [jnp.zeros((samples, 128), jnp.float32) for _ in range(dests)]
        for g0 in range(0, per_key, together):
            rows = jnp.concatenate(
                [own[:, g * HD : (g + 1) * HD] for g in range(g0, g0 + together)], axis=0
            )
            scores = lax.dot_general(
                rows, key, (((1,), (1,)), ((), ())), preferred_element_type=jnp.float32
            ) * HD ** (-0.5)
            high = jnp.max(scores, axis=1, keepdims=True)
            weights = jnp.exp(scores - high)
            total = jnp.sum(weights, axis=1, keepdims=True)
            summed = (
                jnp.dot(weights.astype(jnp.bfloat16), value, preferred_element_type=jnp.float32)
                / total
            )
            lse = high + jnp.log(total)
            for g in range(g0, g0 + together):
                part = slice((g - g0) * samples, (g - g0 + 1) * samples)
                own_lse, other_lse = lse[part], placed_lse[:, g : g + 1]
                top = jnp.maximum(own_lse, other_lse)
                own_weight = jnp.exp(own_lse - top)
                other_weight = jnp.exp(other_lse - top)
                both = own_weight + other_weight
                merged = (
                    own_weight * summed[part]
                    + other_weight * placed[:, g * HD : (g + 1) * HD].astype(jnp.float32)
                ) / both
                at = g % per_dest
                out_mine[j * dests + g // per_dest, :, at * HD : (at + 1) * HD] = merged.astype(
                    jnp.bfloat16
                )
                q = g // per_dest
                tables[q] = jnp.where(lanes_at == at, top + jnp.log(both), tables[q])
        for q in range(dests):
            d = j * dests + q
            lse_mine[d] = tables[q].T[:8]

            @pl.when(d != c)
            def _():
                for copy in piece_copies(c, d):
                    copy.start()

    for k in range(1, n):
        d = lax.rem(c + k, n)
        for copy in piece_copies(d, d):
            copy.wait_recv()
    for k in range(1, n):
        d = lax.rem(c + k, n)
        for copy in piece_copies(c, d):
            copy.wait_send()

    lses = [lse_mine[c]] + [lse_in[lax.rem(c + k, n)] for k in range(1, n)]
    peak = functools.reduce(jnp.maximum, lses)
    scales = [jnp.exp(value - peak) for value in lses]
    denom = functools.reduce(jnp.add, scales)
    blank = jnp.zeros((120, samples), jnp.float32)
    scales = [jnp.concatenate([value / denom, blank], axis=0).T for value in scales]
    for j in range(per_dest):
        lanes = slice(j * HD, (j + 1) * HD)
        total = scales[0][:, j : j + 1] * out_mine[c, :, lanes].astype(jnp.float32)
        for k in range(1, n):
            piece = out_in[lax.rem(c + k, n), :, lanes].astype(jnp.float32)
            total = total + scales[k][:, j : j + 1] * piece
        attn[s, :, lanes] = total.astype(jnp.bfloat16)

    def attn_copy(k):
        return remote(
            attn.at[s], attn.at[s], xs.at[k - 1], xr.at[k - 1], {"smp": lax.rem(s + k, n_smp)}
        )

    for k in range(1, n_smp):
        attn_copy(k).start()
    for k in range(1, n_smp):
        attn_copy(k).wait()

    line = Line(n, c, h, buf_a, recv_a, buf_b, from_left, from_right, sa, ra, ss, rl, rr)

    def gather_copy(t, q, way, sems):
        block = state_ref.at[q, h, :, columns(t, TILE)]
        return remote(
            block, block, sems.at[t, q], gr.at[t, q], {"ctx": lax.rem(c + way, n)}
        )

    def pass_copy(t, q):
        block = state_ref.at[q, h, :, columns(t, TILE)]
        return remote(block, block, fs.at[t, q], fr.at[t, q], {"head": 1 - h})

    def spread(t, q, right, left):
        @pl.when(right & (c < n - 1))
        def _():
            gather_copy(t, q, 1, gsr).start()

        @pl.when(left & (c > 0))
        def _():
            gather_copy(t, q, n - 1, gsl).start()

        pass_copy(t, q).start()

    @pl.loop(0, tiles + 2 * n - 1)
    def _(i):
        @pl.when(i < tiles)
        def _():
            w_copy(i).wait()
            rows = attn[...].reshape(-1, attn.shape[2])
            line.give(i, jnp.dot(rows, w_buf[i], preferred_element_type=jnp.float32))

        line.step(i)

        @pl.when((i >= n) & (i < tiles + n))
        def _():
            t = i - n
            own = line.finish(t) + res_ref[:, columns(t, TILE)].astype(jnp.float32)
            state_ref[c, h, :, columns(t, TILE)] = own.astype(jnp.bfloat16)
            spread(t, c, c >= 0, c >= 0)

        for q in range(n):
            t = i - n - lax.max(c - q, q - c)

            @pl.when((q != c) & (t >= 0) & (t < tiles))
            def _():
                gather_copy(t, q, 1, gsr).wait_recv()
                spread(t, q, q < c, q > c)

    @pl.loop(0, tiles)
    def _(t):
        line.drain(t)
        for q in range(n):

            @pl.when((q <= c) & (c < n - 1))
            def _():
                gather_copy(t, q, 1, gsr).wait_send()

            @pl.when((q >= c) & (c > 0))
            def _():
                gather_copy(t, q, n - 1, gsl).wait_send()

            pass_copy(t, q).wait()


def project(n, n_smp, queries, prefix_cache, suffix_out, suffix_lse, w, residual):
    keys, samples, per_key = suffix_lse.shape
    features = queries.shape[1] // n
    rows, width = residual.shape
    tiles = width // TILE
    vmem = pl.BlockSpec(memory_space=pltpu.VMEM)
    dma = pltpu.SemaphoreType.DMA
    bf16 = jnp.bfloat16
    return pl.pallas_call(
        functools.partial(proj_kernel, n, n_smp),
        out_shape=jax.ShapeDtypeStruct((n, 2, rows, width), bf16),
        in_specs=[vmem, vmem, vmem, vmem, pl.BlockSpec(memory_space=pl.ANY), vmem],
        out_specs=vmem,
        scratch_shapes=[
            pltpu.VMEM((n, samples, features), bf16),
            pltpu.VMEM((n, 8, samples), jnp.float32),
            pltpu.VMEM((n, samples, features), bf16),
            pltpu.VMEM((n, 8, samples), jnp.float32),
            pltpu.VMEM((n_smp, samples, features), bf16),
            pltpu.VMEM((tiles, w.shape[0], TILE), bf16),
            pltpu.VMEM((tiles, 2, n, rows, TILE), bf16),
            pltpu.VMEM((tiles, n, rows, TILE), bf16),
            pltpu.VMEM((tiles, n, rows, TILE), bf16),
            pltpu.VMEM((tiles, n, rows, TILE), bf16),
            pltpu.VMEM((tiles, n, rows, TILE), bf16),
            dma((tiles,)),
            dma((n,)),
            dma((n,)),
            dma((n,)),
            dma((n,)),
            dma((n_smp - 1,)),
            dma((n_smp - 1,)),
            dma((tiles,)),
            dma((tiles,)),
            dma((tiles, n)),
            dma((tiles, n)),
            dma((tiles, n)),
            dma((tiles, n)),
            dma((tiles, n)),
            dma((tiles, n)),
            dma((tiles, n)),
            dma((tiles, n)),
        ],
        compiler_params=pltpu.CompilerParams(
            collective_id=0, has_side_effects=True, vmem_limit_bytes=VMEM_BYTES
        ),
    )(queries, prefix_cache, suffix_out, suffix_lse, w, residual)


UNITS = 256
SLOTS = 4


def ffn_kernel(
    n,
    n_smp,
    state_ref,
    gain_ref,
    gate_ref,
    up_ref,
    down_ref,
    mixed_ref,
    scaled,
    squares,
    squares_in,
    gate_buf,
    up_buf,
    down_buf,
    part,
    part_in,
    hidden,
    buf_a,
    recv_a,
    buf_b,
    recv_b,
    g_sem,
    u_sem,
    d_sem,
    qs,
    qr,
    ps,
    pr,
    hs,
    hr,
    sa,
    ra,
    sb,
    rb,
):
    c, s, h = lax.axis_index("ctx"), lax.axis_index("smp"), lax.axis_index("head")
    steps = part.shape[0]
    slots = gate_buf.shape[0]
    tiles = down_buf.shape[0]
    width = state_ref.shape[3]
    all_rows = state_ref.shape[0] * 2 * state_ref.shape[2]
    smp_rows = all_rows // n_smp

    def weight_copies(t):
        slot = lax.rem(t, slots)
        return (
            pltpu.make_async_copy(
                gate_ref.at[:, columns(t, UNITS)], gate_buf.at[slot], g_sem.at[slot]
            ),
            pltpu.make_async_copy(up_ref.at[:, columns(t, UNITS)], up_buf.at[slot], u_sem.at[slot]),
        )

    def down_copy(t):
        return pltpu.make_async_copy(down_ref.at[:, columns(t, TILE)], down_buf.at[t], d_sem.at[t])

    @pl.loop(0, min(slots, steps))
    def _(t):
        for copy in weight_copies(t):
            copy.start()

    greet(n, n_smp, c, s, h)

    for block in range(n):
        wide = state_ref[block].reshape(-1, width).astype(jnp.float32)
        rows = slice(block * wide.shape[0], (block + 1) * wide.shape[0])
        scaled[rows] = (wide * gain_ref[...]).astype(jnp.bfloat16)
        sums = jnp.sum(wide * wide, axis=1, keepdims=True)
        squares[rows] = jnp.broadcast_to(sums, (wide.shape[0], 128))

    def smp_rows_of(p):
        return pl.ds(pl.multiple_of(p * smp_rows, smp_rows), smp_rows)

    def square_copy(k):
        p = lax.rem(s + k, n_smp)
        return remote(
            squares.at[smp_rows_of(p)], squares_in.at[k - 1], qs.at[k - 1], qr.at[k - 1], {"smp": p}
        )

    for k in range(1, n_smp):
        square_copy(k).start()

    def part_copy(t, k):
        p = lax.rem(s + k, n_smp)
        return remote(
            part.at[t, smp_rows_of(p)],
            part_in.at[t, k - 1],
            ps.at[t, k - 1],
            pr.at[t, k - 1],
            {"smp": p},
        )

    def hidden_copy(t, k):
        block = hidden.at[smp_rows_of(s), columns(t, UNITS)]
        return remote(
            block, block, hs.at[t, k - 1], hr.at[t, k - 1], {"smp": lax.rem(s + k, n_smp)}
        )

    def act(t):
        both = part[t, smp_rows_of(s)].astype(jnp.float32)
        for k in range(1, n_smp):
            part_copy(t, k).wait()
            both = both + part_in[t, k - 1].astype(jnp.float32)
        total = squares[smp_rows_of(s)]
        for k in range(1, n_smp):
            total = total + squares_in[k - 1]
        factor = lax.rsqrt(total / (width * n_smp) + EPSILON)[:, :1]
        gate = factor * both[:, :UNITS]
        up = factor * both[:, UNITS:]
        value = gate / (1.0 + jnp.exp(-gate)) * up
        hidden[smp_rows_of(s), columns(t, UNITS)] = value.astype(jnp.bfloat16)
        for k in range(1, n_smp):
            hidden_copy(t, k).start()

    lag = min(2, steps)

    @pl.loop(0, steps)
    def _(t):
        for copy in weight_copies(t):
            copy.wait()
        slot = lax.rem(t, slots)
        part[t, :, :UNITS] = jnp.dot(
            scaled[...], gate_buf[slot], preferred_element_type=jnp.float32
        ).astype(jnp.bfloat16)
        part[t, :, UNITS:] = jnp.dot(
            scaled[...], up_buf[slot], preferred_element_type=jnp.float32
        ).astype(jnp.bfloat16)
        for k in range(1, n_smp):
            part_copy(t, k).start()

        @pl.when(t + slots < steps)
        def _():
            for copy in weight_copies(t + slots):
                copy.start()

        @pl.when(t < tiles)
        def _():
            down_copy(t).start()

        @pl.when(t == lag)
        def _():
            for k in range(1, n_smp):
                square_copy(k).wait()

        @pl.when(t >= lag)
        def _():
            act(t - lag)

    if steps <= lag:
        for k in range(1, n_smp):
            square_copy(k).wait()

    for t in range(steps, tiles):
        down_copy(t).start()

    @pl.loop(steps - lag, steps)
    def _(t):
        act(t)

    @pl.loop(0, steps)
    def _(t):
        for k in range(1, n_smp):
            hidden_copy(t, k).wait()

    scatter = Scatter(n, c, h, buf_a, recv_a, buf_b, recv_b, sa, ra, sb, rb)

    @pl.loop(0, tiles)
    def _(t):
        down_copy(t).wait()
        scatter.give(t, jnp.dot(hidden[...], down_buf[t], preferred_element_type=jnp.float32))

        @pl.when(t >= 1)
        def _():
            scatter.middle(t - 1)

    scatter.middle(tiles - 1)

    @pl.loop(0, tiles)
    def _(t):
        own = scatter.finish(t) + state_ref[c, h, :, columns(t, TILE)].astype(jnp.float32)
        mixed_ref[:, columns(t, TILE)] = own.astype(jnp.bfloat16)


def feed_forward(n, n_smp, state, gain, gate, up, down):
    _, _, rows, width = state.shape
    all_rows = n * 2 * rows
    smp_rows = all_rows // n_smp
    units = gate.shape[1]
    steps, tiles = units // UNITS, width // TILE
    slots = min(SLOTS, steps)
    vmem = pl.BlockSpec(memory_space=pltpu.VMEM)
    hbm = pl.BlockSpec(memory_space=pl.ANY)
    dma = pltpu.SemaphoreType.DMA
    bf16 = jnp.bfloat16
    return pl.pallas_call(
        functools.partial(ffn_kernel, n, n_smp),
        out_shape=jax.ShapeDtypeStruct((rows, width), bf16),
        in_specs=[vmem, vmem, hbm, hbm, hbm],
        out_specs=vmem,
        scratch_shapes=[
            pltpu.VMEM((all_rows, width), bf16),
            pltpu.VMEM((all_rows, 128), jnp.float32),
            pltpu.VMEM((n_smp - 1, smp_rows, 128), jnp.float32),
            pltpu.VMEM((slots, width, UNITS), bf16),
            pltpu.VMEM((slots, width, UNITS), bf16),
            pltpu.VMEM((tiles, units, TILE), bf16),
            pltpu.VMEM((steps, all_rows, 2 * UNITS), bf16),
            pltpu.VMEM((steps, n_smp - 1, smp_rows, 2 * UNITS), bf16),
            pltpu.VMEM((all_rows, units), bf16),
            pltpu.VMEM((tiles, 2, n, rows, TILE), bf16),
            pltpu.VMEM((tiles, n, rows, TILE), bf16),
            pltpu.VMEM((tiles, n, rows, TILE), bf16),
            pltpu.VMEM((tiles, n - 1, rows, TILE), bf16),
            dma((slots,)),
            dma((slots,)),
            dma((tiles,)),
            dma((n_smp - 1,)),
            dma((n_smp - 1,)),
            dma((steps, n_smp - 1)),
            dma((steps, n_smp - 1)),
            dma((steps, n_smp - 1)),
            dma((steps, n_smp - 1)),
            dma((tiles,)),
            dma((tiles,)),
            dma((tiles, n - 1)),
            dma((tiles, n - 1)),
        ],
        compiler_params=pltpu.CompilerParams(
            collective_id=1, has_side_effects=True, vmem_limit_bytes=VMEM_BYTES
        ),
    )(state, gain, gate, up, down)


def on_device(
    queries,
    prefix_cache,
    suffix_cache,
    suffix_length,
    cache_sample,
    residual,
    w_out,
    norm_gain,
    gate_matrix,
    w_up,
    w_down,
):
    group_rows = queries.shape[0]
    keys_here = prefix_cache.shape[3] // HD
    heads_local = queries.shape[2] // HD
    n, n_smp = lax.axis_size("ctx"), lax.axis_size("smp")
    own_queries = queries[:, 0]
    rows_here = suffix_cache.shape[1]
    flat_index = lax.axis_index("ctx") * n_smp + lax.axis_index("smp")
    row_ids = lax.dynamic_slice_in_dim(cache_sample, flat_index * rows_here, rows_here, 0)
    local_ids = row_ids % group_rows
    row_queries = jnp.take(own_queries, local_ids, axis=0).reshape(rows_here, heads_local, HD)
    row_lengths = jnp.take(suffix_length, local_ids, axis=0)
    suffix_out, suffix_lse = suffix_piece(row_queries, suffix_cache[:, :, :, 0], row_lengths)
    chosen = local_ids[None, :] == jnp.arange(group_rows, dtype=jnp.int32)[:, None]
    placed_out = jnp.dot(
        chosen.astype(jnp.bfloat16),
        suffix_out.reshape(rows_here, -1),
        preferred_element_type=jnp.float32,
    ).astype(jnp.bfloat16)
    placed_lse = jnp.dot(
        chosen.astype(jnp.float32), suffix_lse[:, :, 0], precision=lax.Precision.HIGHEST
    )
    placed_lse = jnp.where(jnp.any(chosen, axis=1)[:, None], placed_lse, -1e30)
    placed_lse = placed_lse.reshape(group_rows, keys_here, -1).transpose(1, 0, 2)
    state = project(
        n,
        n_smp,
        own_queries,
        prefix_cache[:, :, 0],
        placed_out,
        placed_lse,
        w_out[0],
        residual,
    )
    return feed_forward(n, n_smp, state, norm_gain[None, :], gate_matrix, w_up, w_down)


def solution(mesh):
    in_specs = (
        P(("group", "smp"), "head", None),
        P(None, ("group", "ctx"), "head", None),
        P(None, ("group", "ctx", "smp"), None, "head", None),
        P(("group", "smp")),
        P("group"),
        P(("group", "ctx", "head"), "smp"),
        P("head", "ctx", "smp"),
        P("smp"),
        P("smp", ("ctx", "head")),
        P("smp", ("ctx", "head")),
        P(("ctx", "head"), "smp"),
    )
    out_specs = P(("group", "ctx", "head"), "smp")
    return jax.shard_map(
        on_device, mesh=mesh, in_specs=in_specs, out_specs=out_specs, check_vma=False
    )
```
